128 devices in a mesh: frame: 8 (over z_lo, x), head: 16 (over y, z_hi, core).
Axes of the slice: x: 4, y: 4, z: 4 (z_hi: 2, z_lo: 2; z = z_hi * 2 + z_lo), core: 2. Of those that a mesh axis runs over, the one named last changes fastest.
Arguments:
- tokens: float32 [16, 1024, 1024], P('frame', 'head'), may hold values from -48 to 48
- qkv_weight: float32 [1024, 3072], replicated
- out_weight: float32 [1024, 1024], replicated, may hold values from -0.1875 to 0.1875
- norm_gain: float32 [1024], replicated, may hold values from 0.1 to 1.9
- proj_weight: float32 [1024, 256], replicated, may hold values from -0.1875 to 0.1875
- up_weight: bfloat16 [256, 4096], replicated, may hold values from -0.375 to 0.375
- conv_weight: bfloat16 [2, 3, 3, 256, 256], replicated, may hold values from -0.125 to 0.125
- conv_bias: float32 [2, 256], replicated, may hold values from -3 to 3
- block_lists: int32 [128, 26], P('frame'), may hold values from 0 to 127, as said below
- block_counts: int32 [128], P('frame'), may hold values from 1 to 26, as said below
Outputs:
- refined: bfloat16 [16, 128, 128, 256], P('frame', 'head')
The draws below stay inside these ranges and needn't reach their ends.
Inputs may be any that keep to these rules, and one draw needn't show every extreme that they name: `block_lists`: row b names 26 different key blocks and its first entry is block b itself; entries at or after the row's count are padding and are ignored. `block_counts`: some query block in every draw has all 26 entries valid.
All inputs are finite; a program needn't handle non-finite values.
Results may differ from the reference program's by a relative error of at most 0.0057.
Values may be sent and summed in bfloat16 or wider, within the bound.
No kernel may reach another device: no remote copies, remote signals or barrier semaphores. Data moves between devices by JAX's collectives and lax.ppermute only.
A program may use at most 128 MiB of HBM per device.

```python
import math
import jax
import jax.numpy as jnp
from jax import lax

D = 1024
HEADS = 16
CH = 256
GRID = 32
BLOCK = 128
FRAMES = 16
BLOCKS = 128
SLOTS = 26


def draw_tokens(key, part):
    base = jax.random.fold_in(key, 101)
    shape = (FRAMES, GRID * GRID, D)
    values = jax.random.normal(base, shape, jnp.float32)
    return jnp.clip(values, -6.0, 6.0)


def draw_qkv_weight(key, part):
    base = jax.random.fold_in(key, 202)
    head_dim = D // HEADS
    values = jax.random.normal(base, (D, HEADS, 3, head_dim), jnp.float32)
    values = jnp.clip(values, -6.0, 6.0) * D ** (-0.5)
    return values.reshape(D, 3 * D)


def draw_block_lists(key, part):
    base = jax.random.fold_in(key, 303)
    row_keys = jax.random.split(base, BLOCKS)
    others = jax.vmap(lambda row_key: jax.random.permutation(row_key, BLOCKS - 1))(row_keys)
    others = others[:, :SLOTS - 1].astype(jnp.int32)
    own_block = jnp.arange(BLOCKS, dtype=jnp.int32)[:, None]
    others = others + (others >= own_block).astype(jnp.int32)
    return jnp.concatenate([own_block, others], axis=1)


def draw_block_counts(key, part):
    base = jax.random.fold_in(key, 404)
    busy_key, forced_key, count_key = jax.random.split(base, 3)
    frame_flags = jax.random.randint(busy_key, (FRAMES,), 0, 4)
    forced = jax.random.randint(forced_key, (), 0, FRAMES)
    frame_ids = jnp.arange(FRAMES, dtype=jnp.int32)
    busy = (frame_flags == 0) | (frame_ids == forced)
    busy_blocks = jnp.repeat(busy, GRID * GRID // BLOCK, total_repeat_length=BLOCKS)
    light = jax.random.randint(count_key, (BLOCKS,), 1, SLOTS // 3 + 1)
    return jnp.where(busy_blocks, SLOTS, light).astype(jnp.int32)


def scatter_about(rng, extent, scale, most, kind=jnp.bfloat16):
    entries = scale * jax.random.normal(rng, extent, jnp.float32)
    return jnp.clip(entries, min=-most, max=most).astype(kind)


def setup_inputs(seed: int = 0) -> dict:
    arg_keys = jax.random.split(jax.random.key(seed), 11)
    tokens = draw_tokens(jax.random.fold_in(arg_keys[10], 71), 0)
    qkv_weight = draw_qkv_weight(jax.random.fold_in(arg_keys[10], 71), 0)
    out_weight = scatter_about(arg_keys[2], (D, D), D ** -0.5, 0.1875, jnp.float32)
    norm_gain = jnp.clip(1.0 + 0.18 * jax.random.normal(arg_keys[3], (D,), jnp.float32), 0.1, 1.9)
    proj_weight = scatter_about(arg_keys[4], (D, CH), D ** -0.5, 0.1875, jnp.float32)
    up_weight = scatter_about(arg_keys[5], (CH, 16 * CH), CH ** -0.5, 0.375)
    conv_weight = scatter_about(arg_keys[6], (2, 3, 3, CH, CH), (9 * CH) ** -0.5, 0.125)
    conv_bias = scatter_about(arg_keys[7], (2, CH), 0.5, 3.0, jnp.float32)
    block_lists = draw_block_lists(jax.random.fold_in(arg_keys[10], 71), 0)
    block_counts = draw_block_counts(jax.random.fold_in(arg_keys[10], 71), 0)
    return dict(tokens=tokens, qkv_weight=qkv_weight, out_weight=out_weight, norm_gain=norm_gain, proj_weight=proj_weight, up_weight=up_weight, conv_weight=conv_weight, conv_bias=conv_bias, block_lists=block_lists, block_counts=block_counts)


highest = lax.Precision.HIGHEST
eps_norm = 1e-05

def attend(queries, key_values, block_ids, counts, factor):
    groups, slot_total = block_ids.shape
    block_size = queries.shape[1]
    picked = key_values[block_ids]
    picked = picked.reshape((groups, slot_total * block_size) + picked.shape[3:])
    scores = jnp.einsum('gihe,gjhe->ghij', queries, picked[:, :, :, 0, :], precision=highest) * factor
    slot_of = jnp.arange(slot_total * block_size, dtype=jnp.int32) // block_size
    usable = slot_of[None, :] < counts[:, None]
    scores = jnp.where(usable[:, None, None, :], scores, -jnp.inf)
    row_max = lax.optimization_barrier(jnp.max(scores, axis=3, keepdims=True))
    weights = jnp.exp(scores - row_max)
    totals = lax.optimization_barrier(jnp.sum(weights, axis=3))
    blended = jnp.einsum('ghij,gjhe->gihe', weights, picked[:, :, :, 1, :], precision=highest)
    return blended / jnp.transpose(totals, (0, 2, 1))[:, :, :, None]

def layer_norm(rows, gain):
    centre = lax.optimization_barrier(jnp.mean(rows, axis=-1, keepdims=True))
    centred = rows - centre
    spread = lax.optimization_barrier(jnp.mean(centred * centred, axis=-1, keepdims=True))
    return centred * lax.rsqrt(spread + eps_norm) * gain

def conv_window(padded, weight):
    frames_here, rows_in, cols_in, channels = padded.shape
    rows_out = rows_in - 2
    cols_out = cols_in - 2
    summed = jnp.zeros((frames_here * rows_out * cols_out, weight.shape[-1]), jnp.float32)
    for row_off in range(3):
        for col_off in range(3):
            window = padded[:, row_off:row_off + rows_out, col_off:col_off + cols_out, :]
            summed = summed + jnp.dot(window.reshape(-1, channels), weight[row_off, col_off], preferred_element_type=jnp.float32)
    return summed.reshape(frames_here, rows_out, cols_out, -1)

def pad_both(image):
    return jnp.pad(image, ((0, 0), (1, 1), (1, 1), (0, 0)))

def reference(tokens, qkv_weight, out_weight, norm_gain, proj_weight, up_weight, conv_weight, conv_bias, block_lists, block_counts):
    model_width = tokens.shape[2]
    head_dim = model_width // HEADS
    flat_rows = tokens.reshape(-1, model_width)
    packed = jnp.dot(flat_rows, qkv_weight, precision=highest, preferred_element_type=jnp.float32)
    packed = packed.reshape(-1, HEADS, 3, head_dim)
    queries = packed[:, :, 0, :].reshape(-1, BLOCK, HEADS, head_dim)
    key_values = packed[:, :, 1:, :].reshape(-1, BLOCK, HEADS, 2, head_dim)
    block_total = queries.shape[0]
    group_blocks = math.gcd(block_total, max(1, 512 // BLOCK))
    group_count = block_total // group_blocks
    factor = head_dim ** (-0.5)

    def one_group(items):
        return attend(items[0], key_values, items[1], items[2], factor)
    attended = lax.map(one_group, (queries.reshape(group_count, group_blocks, BLOCK, HEADS, head_dim), block_lists.reshape(group_count, group_blocks, -1), block_counts.reshape(group_count, group_blocks)))
    attended = attended.reshape(-1, model_width)
    stream = flat_rows + jnp.dot(attended, out_weight, precision=highest, preferred_element_type=jnp.float32)
    normed = layer_norm(stream, norm_gain)
    features = jnp.dot(normed, proj_weight, precision=highest, preferred_element_type=jnp.float32).astype(jnp.bfloat16)
    channels = features.shape[1]
    lifted = jnp.dot(features, up_weight, preferred_element_type=jnp.float32).astype(jnp.bfloat16)
    lifted = lifted.reshape(-1, GRID, GRID, 4, 4, channels)
    upsampled = jnp.transpose(lifted, (0, 1, 3, 2, 4, 5)).reshape(-1, 4 * GRID, 4 * GRID, channels)
    activated = jnp.maximum(upsampled, jnp.zeros((), jnp.bfloat16))
    first_conv = conv_window(pad_both(activated), conv_weight[0]) + conv_bias[0]
    hidden = jnp.maximum(first_conv, 0.0).astype(jnp.bfloat16)
    second = conv_window(pad_both(hidden), conv_weight[1]) + conv_bias[1]
    return (upsampled.astype(jnp.float32) + second).astype(jnp.bfloat16)
```

```python
import jax
import jax.numpy as jnp
from jax import lax
from jax.experimental import pallas as pl
from jax.experimental.pallas import tpu as pltpu
from jax.sharding import Mesh, PartitionSpec as P

D = 1024
HEADS = 16
HD = 64
CH = 256
SLOTS = 26
STRIP = 64
NEG = -2e38
bf16 = jnp.bfloat16
f32 = jnp.float32


def split(v):
    hi = v.astype(bf16)
    return hi, (v - hi.astype(f32)).astype(bf16)


def dot(a, b):
    return jnp.dot(a, b, preferred_element_type=f32)


def dot3(ah, al, bh, bl):
    return dot(ah, bh) + (dot(al, bh) + dot(ah, bl))


def lanes(shape):
    return lax.broadcasted_iota(jnp.int32, shape, len(shape) - 1)


def qkv_body(x_ref, w_ref, out_ref, xh, xl):
    @pl.when(pl.program_id(0) == 0)
    def _():
        hi, lo = split(x_ref[...])
        xh[...] = hi
        xl[...] = lo

    wh, wl = split(w_ref[...])
    r = dot3(xh[...], xl[...], wh, wl)
    for u in range(2):
        q = r[:, u * 192 : u * 192 + HD] * 0.125
        k = r[:, u * 192 + HD : u * 192 + 2 * HD]
        v = r[:, u * 192 + 2 * HD : u * 192 + 3 * HD]
        for i, t in enumerate((q, k)):
            lo = t - t.astype(bf16).astype(f32)
            out_ref[u, i * 128 : i * 128 + 128, :] = jnp.concatenate([t, lo], axis=1).astype(bf16)
        out_ref[u, 256:320, :] = jnp.concatenate([v[:STRIP], v[STRIP:]], axis=1).astype(bf16)


def qkv(x, w):
    return pl.pallas_call(
        qkv_body,
        grid=(HEADS // 2,),
        in_specs=[
            pl.BlockSpec((128, D), lambda g: (0, 0)),
            pl.BlockSpec((D, 384), lambda g: (0, g)),
        ],
        out_specs=pl.BlockSpec((2, 320, 128), lambda g: (g, 0, 0)),
        out_shape=jax.ShapeDtypeStruct((HEADS, 320, 128), bf16),
        scratch_shapes=[pltpu.VMEM((128, D), bf16), pltpu.VMEM((128, D), bf16)],
        name="qkv",
    )(x, w)


GROUP = 4


def attend_body(ids, cnt, info, kv0, kv1, q0, q1, q2, q3, o_ref, ks, vs, res, ms, accs):
    low = lanes((128, 128)) < HD
    for src, kv in enumerate((kv0, kv1)):

        def keys(j, _):
            for fr in range(2):
                b = src * 16 + fr * 8 + j
                a = jnp.concatenate(
                    [kv[2 * j, fr * 64 : fr * 64 + 64, :], kv[2 * j + 1, fr * 64 : fr * 64 + 64, :]],
                    axis=0,
                )
                ks[b, :, 0:128] = a
                ks[b, :, 128:256] = pltpu.roll(a.astype(f32), 64, 1).astype(bf16)
                v = jnp.concatenate([kv[2 * j, 128:192, :], kv[2 * j + 1, 128:192, :]], axis=0)
                v = v.astype(f32)
                if fr:
                    v = pltpu.roll(v, 64, 1)
                vs[b] = jnp.where(low, v, 1.0).astype(bf16)
            return 0

        lax.fori_loop(0, 8, keys, 0)

    for s, q in enumerate((q0, q1, q2, q3)):

        def group(g, _):
            fr = g // 2
            j0 = (g % 2) * GROUP
            first = s * 16 + g * GROUP
            most = cnt[first]
            for u in range(1, GROUP):
                most = jnp.maximum(most, cnt[first + u])
            trips = jnp.maximum((most + 1) // 2, 1)
            row = pl.multiple_of(fr * 64, 64)
            qs = []
            for u in range(GROUP):
                j = j0 + u
                a = jnp.concatenate(
                    [q[2 * j, pl.ds(row, 64), :], q[2 * j + 1, pl.ds(row, 64), :]], axis=0
                )
                qs.append(jnp.concatenate([a, a], axis=1))
                ms[u] = jnp.full((128, 128), NEG, f32)
                accs[u] = jnp.zeros((128, 128), f32)

            def step(t, _):
                for u in range(GROUP):
                    b = first + u
                    ia = ids[b, 2 * t]
                    ib = ids[b, 2 * t + 1]
                    kk = jnp.concatenate([ks[ia], ks[ib]], axis=0)
                    vv = jnp.concatenate([vs[ia], vs[ib]], axis=0)
                    sc = lax.dot_general(
                        qs[u], kk, (((1,), (1,)), ((), ())), preferred_element_type=f32
                    )
                    sa = jnp.where(2 * t < cnt[b], sc[:, :128], NEG)
                    sb = jnp.where(2 * t + 1 < cnt[b], sc[:, 128:], NEG)
                    old = ms[u]
                    new = jnp.maximum(old, jnp.max(jnp.maximum(sa, sb), axis=1, keepdims=True))
                    p = jnp.concatenate([jnp.exp(sa - new), jnp.exp(sb - new)], axis=1)
                    accs[u] = accs[u] * jnp.exp(old - new) + dot(p.astype(bf16), vv)
                    ms[u] = new
                return 0

            lax.fori_loop(0, trips, step, 0)
            for u in range(GROUP):
                acc = accs[u]
                total = jnp.where(low, pltpu.roll(acc, 64, 1), acc)
                res[fr * 8 + j0 + u] = jnp.where(low, acc / total, ms[u] + jnp.log(total))
            return 0

        lax.fori_loop(0, 4, group, 0)
        to = info[s]

        def emit(j, _):
            r0 = res[j]
            r1 = res[8 + j]
            out = jnp.where(low, r0, pltpu.roll(r1, 64, 1)).astype(bf16)
            t0 = r0.T[HD : HD + 1, :]
            t1 = r1.T[HD : HD + 1, :]
            sub = lax.broadcasted_iota(jnp.int32, (16, 128), 0)
            for half in range(2):
                o_ref[to, 2 * j + half, 0:64, :] = out[half * 64 : half * 64 + 64]
                c = half * 64
                row = jnp.concatenate([t0[:, c : c + 64], t1[:, c : c + 64]], axis=1)
                hi = row.astype(bf16).astype(f32)
                mid = (row - hi).astype(bf16).astype(f32)
                last = row - hi - mid
                tile = jnp.where(sub == 0, hi, jnp.where(sub == 1, mid, jnp.where(sub == 2, last, 0.0)))
                o_ref[to, 2 * j + half, 64:80, :] = tile.astype(bf16)
            return 0

        lax.fori_loop(0, 8, emit, 0)


def attend(ids, cnt, info, kv0, kv1, qs):
    smem = pl.BlockSpec(memory_space=pltpu.SMEM)
    vmem = pl.BlockSpec(memory_space=pltpu.VMEM)
    return pl.pallas_call(
        attend_body,
        in_specs=[smem, smem, smem] + [vmem] * 6,
        out_specs=vmem,
        out_shape=jax.ShapeDtypeStruct((4, HEADS, 80, 128), bf16),
        scratch_shapes=[
            pltpu.VMEM((32, 128, 256), bf16),
            pltpu.VMEM((32, 128, 128), bf16),
            pltpu.VMEM((16, 128, 128), f32),
            pltpu.VMEM((GROUP, 128, 128), f32),
            pltpu.VMEM((GROUP, 128, 128), f32),
        ],
        name="attend",
    )(ids, cnt, info, kv0, kv1, *qs)


def mix_body(r_ref, x_ref, w_ref, gain_ref, proj_ref, feat_ref, top_ref, bot_ref, att):
    lse = jnp.sum(r_ref[:, 64:80, :].astype(f32), axis=1)
    parts = [lse[16 * x : 16 * x + 16] for x in range(4)]
    peak = jnp.maximum(jnp.maximum(parts[0], parts[1]), jnp.maximum(parts[2], parts[3]))
    es = [jnp.exp(p - peak) for p in parts]
    total = (es[0] + es[1]) + (es[2] + es[3])
    share = jnp.concatenate([e / total for e in es], axis=0)
    share = jnp.concatenate([share, share], axis=0).T
    both = jnp.where(lanes((STRIP, 128)) < 64, share[:STRIP], share[STRIP:])
    bh, bl = split(both)
    low = lanes((STRIP, 128)) < HD
    row = lax.broadcasted_iota(jnp.int32, (128, 2048), 0)
    col = lanes((128, 2048))
    half = ((row >= 64) == (col % 128 >= 64)) & True
    wide = []
    for x in range(4):
        spread = jnp.where(half & (row % 64 == 16 * x + col // 128), 1.0, 0.0).astype(bf16)
        wide.append(dot(bh, spread) + dot(bl, spread))
    for p in range(HEADS // 2):
        t = []
        for h in (2 * p, 2 * p + 1):
            acc = None
            for x in range(4):
                o = r_ref[16 * x + h, 0:64, :].astype(f32) * wide[x][:, 128 * h : 128 * h + 128]
                acc = o if acc is None else acc + o
            t.append(acc)
        att[0:64, 128 * p : 128 * p + 128] = jnp.where(low, t[0], pltpu.roll(t[1], 64, 1))
        att[64:128, 128 * p : 128 * p + 128] = jnp.where(low, pltpu.roll(t[0], 64, 1), t[1])
    ah, al = split(att[...])
    wh, wl = split(w_ref[...])
    stream = x_ref[...] + dot3(ah, al, wh, wl)
    centred = stream - jnp.mean(stream, axis=1, keepdims=True)
    spread = jnp.mean(centred * centred, axis=1, keepdims=True)
    normed = centred * lax.rsqrt(spread + 1e-05) * gain_ref[...]
    nh, nl = split(normed)
    ph, plo = split(proj_ref[...])
    feat = dot3(nh, nl, ph, plo).astype(bf16)
    feat_ref[...] = feat
    for f in range(2):
        top_ref[32 * f : 32 * f + 32] = feat[64 * f : 64 * f + 32]
        bot_ref[32 * f : 32 * f + 32] = feat[64 * f + 32 : 64 * f + 64]


def mix(r, x, w, gain, proj):
    return pl.pallas_call(
        mix_body,
        out_shape=(
            jax.ShapeDtypeStruct((128, CH), bf16),
            jax.ShapeDtypeStruct((64, CH), bf16),
            jax.ShapeDtypeStruct((64, CH), bf16),
        ),
        scratch_shapes=[pltpu.VMEM((128, D), f32)],
        name="mix",
    )(r, x, w, gain, proj)


def shifted(dst, src, rows, relu):
    def one(r, _):
        for dx in range(3):
            for half in range(2):
                v = src[half * rows + r, pl.ds(7 + dx, 128), :]
                if relu:
                    v = jnp.maximum(v, 0.0)
                dst[r, :, dx * 256 + half * 128 : dx * 256 + half * 128 + 128] = v.astype(bf16)
        return 0

    lax.fori_loop(0, rows, one, 0)


def head_body(pos, feat_ref, above_ref, below_ref, up_ref, cw_ref, cb_ref, out_ref, ups, u3, hid, h3):
    at = pos[0]

    @pl.when(pl.program_id(0) == 0)
    def _():
        for ref, rows in ((ups, 24), (hid, 20)):
            ref[:, 0:8, :] = jnp.zeros((rows, 8, 128), f32)
            ref[:, 136:144, :] = jnp.zeros((rows, 8, 128), f32)

    own = feat_ref[...]
    early = jnp.concatenate([own, below_ref[...]], axis=0)
    late = jnp.concatenate([above_ref[...], own], axis=0)
    for a in range(4):
        src = early if a < 2 else late
        lifted = dot(src, up_ref[:, 1024 * a : 1024 * a + 1024]).astype(bf16).astype(f32)
        for i in range(3):
            row = 2 + 4 * i + a if a < 2 else 4 * i + a - 2
            for e in range(4):
                for half in range(2):
                    c = 256 * e + 128 * half
                    ups[12 * half + row, pl.ds(8 + e, 32, stride=4), :] = lifted[
                        32 * i : 32 * i + 32, c : c + 128
                    ]
    shifted(u3, ups, 12, True)

    def conv1(r, _):
        acc = None
        for dy in range(3):
            part = dot(u3[pl.ds(2 * r + dy, 2)].reshape(256, 768), cw_ref[0, dy])
            acc = part if acc is None else acc + part
        h = jnp.maximum(acc + cb_ref[0:1, :], 0.0).astype(bf16).astype(f32)
        for k in range(2):
            y = 2 * r + k
            keep = ((y > 0) | (at > 0)) & ((y < 9) | (at < 15))
            v = jnp.where(keep, h[128 * k : 128 * k + 128], 0.0)
            for half in range(2):
                hid[10 * half + y, 8:136, :] = v[:, 128 * half : 128 * half + 128]
        return 0

    lax.fori_loop(0, 5, conv1, 0)
    shifted(h3, hid, 10, False)

    def conv2(r, _):
        acc = None
        for dy in range(3):
            part = dot(h3[pl.ds(2 * r + dy, 2)].reshape(256, 768), cw_ref[1, dy])
            acc = part if acc is None else acc + part
        acc = acc + cb_ref[1:2, :]
        for k in range(2):
            y = 2 * r + k
            for half in range(2):
                c = 128 * half
                v = ups[12 * half + y + 2, 8:136, :] + acc[128 * k : 128 * k + 128, c : c + 128]
                out_ref[0, y, :, c : c + 128] = v.astype(bf16)
        return 0

    lax.fori_loop(0, 4, conv2, 0)


def dense_head(pos, feat, above, below, up, cw, cb):
    whole = lambda shape: pl.BlockSpec(shape, lambda f: (0,) * len(shape))
    return pl.pallas_call(
        head_body,
        grid=(2,),
        in_specs=[
            pl.BlockSpec(memory_space=pltpu.SMEM),
            pl.BlockSpec((64, CH), lambda f: (f, 0)),
            pl.BlockSpec((32, CH), lambda f: (f, 0)),
            pl.BlockSpec((32, CH), lambda f: (f, 0)),
            whole((CH, 16 * CH)),
            whole((2, 3, 3 * CH, CH)),
            whole((2, CH)),
        ],
        out_specs=pl.BlockSpec((1, 8, 128, CH), lambda f: (f, 0, 0, 0)),
        out_shape=jax.ShapeDtypeStruct((2, 8, 128, CH), bf16),
        scratch_shapes=[
            pltpu.VMEM((24, 144, 128), f32),
            pltpu.VMEM((12, 128, 768), bf16),
            pltpu.VMEM((20, 144, 128), f32),
            pltpu.VMEM((10, 128, 768), bf16),
        ],
        name="dense_head",
    )(pos, feat, above, below, up, cw, cb)


def local_lists(lists, counts, x, z):
    packed = jnp.concatenate([lists, counts[:, None]], axis=1)
    sets = [packed] + [
        lax.ppermute(packed, "x", [(i, (i + k) % 4) for i in range(4)]) for k in (1, 2, 3)
    ]
    packed = jnp.concatenate(sets, axis=0)
    ids = packed[:, :SLOTS]
    slot = jnp.arange(SLOTS, dtype=jnp.int32)
    mine = (slot[None, :] < packed[:, SLOTS:]) & ((ids // 16) % 4 == x)
    local = jnp.where(ids // 64 == z, 0, 16) + ids % 16
    before = jnp.sum(
        jnp.where(mine[:, None, :] & (slot[None, None, :] < slot[None, :, None]), 1, 0), axis=2
    )
    place = mine[:, None, :] & (before[:, None, :] == slot[None, :, None])
    ids = jnp.sum(jnp.where(place, local[:, None, :], 0), axis=2)
    return ids.astype(jnp.int32), jnp.sum(mine, axis=1).astype(jnp.int32)


def on_device(tokens, qkv_w, out_w, gain, proj_w, up_w, conv_w, conv_b, lists, counts):
    x = lax.axis_index("x")
    z = lax.axis_index("z")
    strip = lax.axis_index("head")
    flat = tokens.reshape(-1, D)
    ids, cnt = local_lists(lists, counts, x, z)
    packed = qkv(flat, qkv_w)
    packed = lax.all_to_all(packed, "head", split_axis=0, concat_axis=0, tiled=True)
    q = packed[:, :128]
    kv = packed[:, 128:]
    kv_far = lax.ppermute(kv, "z", [(0, 1), (1, 0)])
    qs = [q] + [lax.ppermute(q, "x", [(i, (i + k) % 4) for i in range(4)]) for k in (1, 2, 3)]
    info = (x - jnp.arange(4, dtype=jnp.int32)) % 4
    part = attend(ids, cnt, info, kv, kv_far, qs)
    part = lax.all_to_all(
        part.reshape(64, 80, 128), ("x", "head"), split_axis=0, concat_axis=0, tiled=True
    )
    feat, top, bot = mix(part, flat, out_w, gain[None, :], proj_w)
    above = lax.ppermute(bot, "head", [(i, i + 1) for i in range(15)])
    below = lax.ppermute(top, "head", [(i + 1, i) for i in range(15)])
    return dense_head(
        strip[None], feat, above, below, up_w, conv_w.reshape(2, 3, 3 * CH, CH), conv_b
    )


def solution(mesh):
    grid = Mesh(mesh.devices.reshape(2, 4, 16), ("z", "x", "head"))
    rows = ("z", "x")
    in_specs = (
        P(rows, "head", None),
        P(),
        P(),
        P(),
        P(),
        P(),
        P(),
        P(),
        P(rows, None),
        P(rows),
    )
    return jax.shard_map(
        on_device,
        mesh=grid,
        in_specs=in_specs,
        out_specs=P(rows, "head", None, None),
        check_vma=False,
    )
```

```python
import functools

import jax
import jax.numpy as jnp
from jax import lax
from jax.experimental import pallas as pl
from jax.experimental.pallas import tpu as pltpu
from jax.sharding import Mesh, PartitionSpec as P

D = 1024
HEADS = 16
HD = 64
CH = 256
SLOTS = 26
STRIP = 64
NEG = -2e38
bf16 = jnp.bfloat16
f32 = jnp.float32


def split(v):
    hi = v.astype(bf16)
    return hi, (v - hi.astype(f32)).astype(bf16)


def dot(a, b):
    return jnp.dot(a, b, preferred_element_type=f32)


def dot3(ah, al, bh, bl):
    m = ah.shape[0]
    both = dot(jnp.concatenate([ah, al], axis=0), bh)
    return both[:m] + (both[m:] + dot(ah, bl))


def lanes(shape):
    return lax.broadcasted_iota(jnp.int32, shape, len(shape) - 1)


def qkv_body(x_ref, w_ref, out_ref, xh, xl):
    @pl.when(pl.program_id(0) == 0)
    def _():
        hi, lo = split(x_ref[...])
        xh[...] = hi
        xl[...] = lo

    wh, wl = split(w_ref[...])
    r = dot3(xh[...], xl[...], wh, wl)
    for u in range(2):
        q = r[:, u * 192 : u * 192 + HD] * 0.125
        k = r[:, u * 192 + HD : u * 192 + 2 * HD]
        v = r[:, u * 192 + 2 * HD : u * 192 + 3 * HD]
        for i, t in enumerate((q, k)):
            lo = t - t.astype(bf16).astype(f32)
            out_ref[u, i * 128 : i * 128 + 128, :] = jnp.concatenate([t, lo], axis=1).astype(bf16)
        out_ref[u, 256:320, :] = jnp.concatenate([v[:STRIP], v[STRIP:]], axis=1).astype(bf16)


def qkv(x, w):
    return pl.pallas_call(
        qkv_body,
        grid=(HEADS // 2,),
        in_specs=[
            pl.BlockSpec((128, D), lambda g: (0, 0)),
            pl.BlockSpec((D, 384), lambda g: (0, g)),
        ],
        out_specs=pl.BlockSpec((2, 320, 128), lambda g: (g, 0, 0)),
        out_shape=jax.ShapeDtypeStruct((HEADS, 320, 128), bf16),
        scratch_shapes=[pltpu.VMEM((128, D), bf16), pltpu.VMEM((128, D), bf16)],
        name="qkv",
    )(x, w)


UNROLL = 8
PAIRS = 16 * (SLOTS // 2)
ROOM = PAIRS + UNROLL


def attend_body(sets, items, cnt, info, kv0, kv1, *refs):
    qrefs, (o_ref, ks, vs, qs, sc, ms, accs) = refs[:-7], refs[-7:]
    low = lanes((128, 128)) < HD

    def strips(ref, j, rows):
        return jnp.concatenate([ref[2 * j, rows, :], ref[2 * j + 1, rows, :]], axis=0)

    def ready(j, _):
        for fr in range(2):
            rows = slice(fr * 64, fr * 64 + 64)
            for src, kv in enumerate((kv0, kv1)):
                b = src * 16 + fr * 8 + j
                a = strips(kv, j, rows).astype(f32)
                swapped = pltpu.roll(a, 64, 1)
                ks[b, :, 0:128] = jnp.where(low, a, swapped).astype(bf16)
                ks[b, :, 128:256] = swapped.astype(bf16)
                v = strips(kv, j, slice(128, 192)).astype(f32)
                if fr:
                    v = pltpu.roll(v, 64, 1)
                vs[b] = jnp.where(low, v, 1.0).astype(bf16)
        return 0

    lax.fori_loop(0, 8, ready, 0)

    for i in range(len(sets)):
        mine = (qrefs[i],) if len(sets) > 1 else qrefs
        for part, q in enumerate(mine):

            def ready_q(j, _, i=i, part=part, q=q):
                for fr in range(2):
                    rows = slice(fr * 64, fr * 64 + 64)
                    qs[17 * i + fr * 8 + 4 * part + j] = strips(q, j, rows)
                return 0

            lax.fori_loop(0, 8 // len(mine), ready_q, 0)
        qs[17 * i + 16] = jnp.zeros((128, 128), bf16)
    vs[32] = jnp.zeros((128, 128), bf16)
    eye = lax.broadcasted_iota(jnp.int32, (128, 128), 0) == lanes((128, 128))

    def one_set(i, _):
        s = sets[0]
        for n in range(1, len(sets)):
            s = jnp.where(i == n, sets[n], s)
        trips = (cnt[s] + UNROLL - 1) // UNROLL

        def clear(b, _):
            ms[b] = jnp.full((128, 128), NEG, f32)
            accs[b] = jnp.zeros((128, 128), f32)
            return 0

        lax.fori_loop(0, 17, clear, 0)

        def score(t, _):
            got = []
            for u in range(UNROLL):
                item = items[s, t * UNROLL + u]
                ia = (item >> 6) & 31
                ib = item & 63
                a = qs[17 * i + (item >> 11)]
                got.append(
                    lax.dot_general(
                        jnp.concatenate([a, a[:, :HD]], axis=1),
                        jnp.concatenate(
                            [ks[ia, :, :192], ks[jnp.where(ib == 32, ia, ib), :, :192]], axis=0
                        ),
                        (((1,), (1,)), ((), ())),
                        preferred_element_type=f32,
                    )
                )
            for u in range(UNROLL):
                qi = items[s, t * UNROLL + u] >> 11
                sc[t * UNROLL + u] = got[u]
                ms[qi] = jnp.maximum(ms[qi], jnp.maximum(got[u][:, :128], got[u][:, 128:]))
            return 0

        lax.fori_loop(0, trips, score, 0)

        def peak(b, _):
            for u in range(4):
                m = jnp.max(ms[4 * b + u], axis=1, keepdims=True)
                ms[4 * b + u] = jnp.broadcast_to(m, (128, 128))
            return 0

        lax.fori_loop(0, 4, peak, 0)

        def blend(t, _):
            got = []
            for u in range(UNROLL):
                item = items[s, t * UNROLL + u]
                m = ms[item >> 11]
                p = jnp.exp(sc[t * UNROLL + u] - jnp.concatenate([m, m], axis=1))
                v = jnp.concatenate([vs[(item >> 6) & 31], vs[item & 63]], axis=0)
                got.append(dot(p.astype(bf16), v))
            for u in range(UNROLL):
                qi = items[s, t * UNROLL + u] >> 11
                accs[qi] = accs[qi] + got[u]
            return 0

        lax.fori_loop(0, trips, blend, 0)
        to = info[s] if len(sets) > 1 else 0

        def diagonal(v):
            return jnp.sum(jnp.where(eye, v, 0.0), axis=0, keepdims=True)

        def emit(jj, _):
            emit_one(2 * jj)
            emit_one(2 * jj + 1)
            return 0

        def emit_one(j):
            a0 = accs[j]
            a1 = accs[8 + j]
            s0 = pltpu.roll(a0, 64, 1)
            s1 = pltpu.roll(a1, 64, 1)
            total = jnp.maximum(jnp.where(low, s0, a1), 0.5)
            out = (jnp.where(low, a0, s1) / total).astype(bf16)
            l0 = jnp.maximum(diagonal(jnp.where(low, s0, a0)), 0.5)
            l1 = jnp.maximum(diagonal(jnp.where(low, s1, a1)), 0.5)
            t0 = diagonal(ms[j]) + jnp.log(l0)
            t1 = diagonal(ms[8 + j]) + jnp.log(l1)
            sub = lax.broadcasted_iota(jnp.int32, (16, 128), 0)
            for half in range(2):
                o_ref[to, 2 * j + half, 0:64, :] = out[half * 64 : half * 64 + 64]
                c = half * 64
                row = jnp.concatenate([t0[:, c : c + 64], t1[:, c : c + 64]], axis=1)
                hi = row.astype(bf16).astype(f32)
                mid = (row - hi).astype(bf16).astype(f32)
                last = row - hi - mid
                tile = jnp.where(
                    sub == 0, hi, jnp.where(sub == 1, mid, jnp.where(sub == 2, last, 0.0))
                )
                o_ref[to, 2 * j + half, 64:80, :] = tile.astype(bf16)

        lax.fori_loop(0, 4, emit, 0)
        return 0

    lax.fori_loop(0, len(sets), one_set, 0)


def attend(sets, items, cnt, info, kv0, kv1, qs):
    smem = pl.BlockSpec(memory_space=pltpu.SMEM)
    vmem = pl.BlockSpec(memory_space=pltpu.VMEM)
    return pl.pallas_call(
        functools.partial(attend_body, sets),
        in_specs=[smem, smem, smem] + [vmem] * (2 + len(qs)),
        out_specs=vmem,
        out_shape=jax.ShapeDtypeStruct((4 if len(sets) > 1 else 1, HEADS, 80, 128), bf16),
        scratch_shapes=[
            pltpu.VMEM((32, 128, 256), bf16),
            pltpu.VMEM((33, 128, 128), bf16),
            pltpu.VMEM((17 * len(sets), 128, 128), bf16),
            pltpu.VMEM((ROOM, 128, 256), f32),
            pltpu.VMEM((17, 128, 128), f32),
            pltpu.VMEM((17, 128, 128), f32),
        ],
        compiler_params=pltpu.CompilerParams(vmem_limit_bytes=44 << 20),
        name=f"attend_{len(sets)}",
    )(items, cnt, info, kv0, kv1, *qs)


def mix_body(r_ref, x_ref, w_ref, gain_ref, proj_ref, feat_ref, top_ref, bot_ref, att):
    lse = jnp.sum(r_ref[:, 64:80, :].astype(f32), axis=1)
    parts = [lse[16 * x : 16 * x + 16] for x in range(4)]
    peak = jnp.maximum(jnp.maximum(parts[0], parts[1]), jnp.maximum(parts[2], parts[3]))
    es = [jnp.exp(p - peak) for p in parts]
    total = (es[0] + es[1]) + (es[2] + es[3])
    share = jnp.concatenate([e / total for e in es], axis=0)
    share = jnp.concatenate([share, share], axis=0).T
    both = jnp.where(lanes((STRIP, 128)) < 64, share[:STRIP], share[STRIP:])
    bh, bl = split(both)
    low = lanes((STRIP, 128)) < HD
    row = lax.broadcasted_iota(jnp.int32, (128, 2048), 0)
    col = lanes((128, 2048))
    half = (row >= 64) == (col % 128 >= 64)
    wide = []
    for x in range(4):
        spread = jnp.where(half & (row % 64 == 16 * x + col // 128), 1.0, 0.0).astype(bf16)
        wide.append(dot(bh, spread) + dot(bl, spread))
    for p in range(HEADS // 2):
        t = []
        for h in (2 * p, 2 * p + 1):
            acc = None
            for x in range(4):
                o = r_ref[16 * x + h, 0:64, :].astype(f32) * wide[x][:, 128 * h : 128 * h + 128]
                acc = o if acc is None else acc + o
            t.append(acc)
        att[0:64, 128 * p : 128 * p + 128] = jnp.where(low, t[0], pltpu.roll(t[1], 64, 1))
        att[64:128, 128 * p : 128 * p + 128] = jnp.where(low, pltpu.roll(t[0], 64, 1), t[1])
    ah, al = split(att[...])
    wh, wl = split(w_ref[...])
    stream = x_ref[...] + dot3(ah, al, wh, wl)
    centred = stream - jnp.mean(stream, axis=1, keepdims=True)
    spread = jnp.mean(centred * centred, axis=1, keepdims=True)
    normed = centred * lax.rsqrt(spread + 1e-05) * gain_ref[...]
    nh, nl = split(normed)
    ph, plo = split(proj_ref[...])
    feat = dot3(nh, nl, ph, plo).astype(bf16)
    feat_ref[...] = feat
    for f in range(2):
        top_ref[32 * f : 32 * f + 32] = feat[64 * f : 64 * f + 32]
        bot_ref[32 * f : 32 * f + 32] = feat[64 * f + 32 : 64 * f + 64]


def mix(r, x, w, gain, proj):
    return pl.pallas_call(
        mix_body,
        out_shape=(
            jax.ShapeDtypeStruct((128, CH), bf16),
            jax.ShapeDtypeStruct((64, CH), bf16),
            jax.ShapeDtypeStruct((64, CH), bf16),
        ),
        scratch_shapes=[pltpu.VMEM((128, D), f32)],
        compiler_params=pltpu.CompilerParams(vmem_limit_bytes=20 << 20),
        name="mix",
    )(r, x, w, gain, proj)


def shifted(dst, src, rows, relu):
    def one(r, _):
        for dx in range(3):
            for half in range(2):
                v = src[half * rows + r, pl.ds(7 + dx, 128), :]
                if relu:
                    v = jnp.maximum(v, 0.0)
                dst[r, :, dx * 256 + half * 128 : dx * 256 + half * 128 + 128] = v.astype(bf16)
        return 0

    lax.fori_loop(0, rows, one, 0)


def head_body(pos, feat_ref, above_ref, below_ref, up_ref, cw_ref, cb_ref, out_ref, ups, u3, hid, h3):
    at = pos[0]

    @pl.when(pl.program_id(0) == 0)
    def _():
        for ref, rows in ((ups, 24), (hid, 20)):
            ref[:, 0:8, :] = jnp.zeros((rows, 8, 128), f32)
            ref[:, 136:144, :] = jnp.zeros((rows, 8, 128), f32)

    own = feat_ref[...]
    early = jnp.concatenate([own, below_ref[...]], axis=0)
    late = jnp.concatenate([above_ref[...], own], axis=0)
    for a in range(4):
        src = early if a < 2 else late
        lifted = dot(src, up_ref[:, 1024 * a : 1024 * a + 1024]).astype(bf16).astype(f32)
        for i in range(3):
            row = 2 + 4 * i + a if a < 2 else 4 * i + a - 2
            for e in range(4):
                for half in range(2):
                    c = 256 * e + 128 * half
                    ups[12 * half + row, pl.ds(8 + e, 32, stride=4), :] = lifted[
                        32 * i : 32 * i + 32, c : c + 128
                    ]
    shifted(u3, ups, 12, True)

    def conv1(r, _):
        acc = None
        for dy in range(3):
            part = dot(u3[pl.ds(2 * r + dy, 2)].reshape(256, 768), cw_ref[0, dy])
            acc = part if acc is None else acc + part
        h = jnp.maximum(acc + cb_ref[0:1, :], 0.0).astype(bf16).astype(f32)
        for k in range(2):
            y = 2 * r + k
            keep = ((y > 0) | (at > 0)) & ((y < 9) | (at < 15))
            v = jnp.where(keep, h[128 * k : 128 * k + 128], 0.0)
            for half in range(2):
                hid[10 * half + y, 8:136, :] = v[:, 128 * half : 128 * half + 128]
        return 0

    lax.fori_loop(0, 5, conv1, 0)
    shifted(h3, hid, 10, False)

    def conv2(r, _):
        acc = None
        for dy in range(3):
            part = dot(h3[pl.ds(2 * r + dy, 2)].reshape(256, 768), cw_ref[1, dy])
            acc = part if acc is None else acc + part
        acc = acc + cb_ref[1:2, :]
        for k in range(2):
            y = 2 * r + k
            for half in range(2):
                c = 128 * half
                v = ups[12 * half + y + 2, 8:136, :] + acc[128 * k : 128 * k + 128, c : c + 128]
                out_ref[0, y, :, c : c + 128] = v.astype(bf16)
        return 0

    lax.fori_loop(0, 4, conv2, 0)


def dense_head(pos, feat, above, below, up, cw, cb):
    whole = lambda shape: pl.BlockSpec(shape, lambda f: (0,) * len(shape))
    return pl.pallas_call(
        head_body,
        grid=(2,),
        in_specs=[
            pl.BlockSpec(memory_space=pltpu.SMEM),
            pl.BlockSpec((64, CH), lambda f: (f, 0)),
            pl.BlockSpec((32, CH), lambda f: (f, 0)),
            pl.BlockSpec((32, CH), lambda f: (f, 0)),
            whole((CH, 16 * CH)),
            whole((2, 3, 3 * CH, CH)),
            whole((2, CH)),
        ],
        out_specs=pl.BlockSpec((1, 8, 128, CH), lambda f: (f, 0, 0, 0)),
        out_shape=jax.ShapeDtypeStruct((2, 8, 128, CH), bf16),
        scratch_shapes=[
            pltpu.VMEM((24, 144, 128), f32),
            pltpu.VMEM((12, 128, 768), bf16),
            pltpu.VMEM((20, 144, 128), f32),
            pltpu.VMEM((10, 128, 768), bf16),
        ],
        compiler_params=pltpu.CompilerParams(vmem_limit_bytes=24 << 20),
        name="dense_head",
    )(pos, feat, above, below, up, cw, cb)


def local_items(lists, counts, x, z):
    packed = jnp.concatenate([lists, counts[:, None]], axis=1)
    sets = [packed] + [
        lax.ppermute(packed, "x", [(i, (i + k) % 4) for i in range(4)]) for k in (1, 2, 3)
    ]
    packed = jnp.stack(sets, axis=0)
    ids = packed[:, :, :SLOTS]
    slot = jnp.arange(SLOTS, dtype=jnp.int32)
    block = jnp.arange(16, dtype=jnp.int32)
    mine = (slot < packed[:, :, SLOTS:]) & ((ids // 16) % 4 == x)
    local = jnp.where(ids // 64 == z, 0, 16) + ids % 16
    ones = mine.astype(jnp.int32)
    inside = jnp.sum(jnp.where(slot[None, :] < slot[:, None], ones[:, :, None, :], 0), axis=-1)
    total = jnp.sum(ones, axis=-1)
    pairs = (total + 1) // 2
    ahead = jnp.sum(jnp.where(block[None, :] < block[:, None], pairs[:, None, :], 0), axis=-1)
    place = jnp.where(mine, ahead[:, :, None] + inside // 2, -1).reshape(4, 1, -1)
    alone = jnp.where(inside + 1 == total[:, :, None], 32, 0)
    value = jnp.where(inside % 2 == 0, block[:, None] * 2048 + local * 64 + alone, local)
    at = jnp.arange(ROOM, dtype=jnp.int32)[:, None]
    items = jnp.sum(jnp.where(place == at, value.reshape(4, 1, -1), 0), axis=-1)
    count = jnp.sum(pairs, axis=-1)
    items = jnp.where(at[:, 0] < count[:, None], items, 16 * 2048 + 32)
    return items, count


def on_device(tokens, qkv_w, out_w, gain, proj_w, up_w, conv_w, conv_b, lists, counts):
    x = lax.axis_index("x")
    z = lax.axis_index("z")
    strip = lax.axis_index("head")
    flat = tokens.reshape(-1, D)
    right = [(i, (i + 1) % 4) for i in range(4)]
    left = [(i, (i - 1) % 4) for i in range(4)]
    packed = qkv(flat, qkv_w)
    packed, lists, counts = lax.optimization_barrier((packed, lists, counts))
    items, cnt = local_items(lists, counts, x, z)
    packed = lax.all_to_all(packed, "head", split_axis=0, concat_axis=0, tiled=True)
    q = packed[:, :128]
    kv = packed[:, 128:]
    q1 = lax.ppermute(q, "x", right)
    q3 = lax.ppermute(q, "x", left)
    kv_far = lax.ppermute(kv, "z", [(0, 1), (1, 0)])
    q2a = lax.ppermute(q1[:8], "x", right)
    q2b = lax.ppermute(q3[8:], "x", left)
    info = (x - jnp.arange(4, dtype=jnp.int32)) % 4
    part = attend((0, 1, 3), items, cnt, info, kv, kv_far, [q, q1, q3])
    last = attend((2,), items, cnt, info, kv, kv_far, [q2a, q2b])
    part = lax.dynamic_update_slice_in_dim(part, last, info[2], 0)
    part = lax.all_to_all(
        part.reshape(64, 80, 128), ("x", "head"), split_axis=0, concat_axis=0, tiled=True
    )
    feat, top, bot = mix(part, flat, out_w, gain[None, :], proj_w)
    above = lax.ppermute(bot, "head", [(i, i + 1) for i in range(15)])
    below = lax.ppermute(top, "head", [(i + 1, i) for i in range(15)])
    return dense_head(
        strip[None], feat, above, below, up_w, conv_w.reshape(2, 3, 3 * CH, CH), conv_b
    )


def solution(mesh):
    grid = Mesh(mesh.devices.reshape(2, 4, 16), ("z", "x", "head"))
    rows = ("z", "x")
    in_specs = (
        P(rows, "head", None),
        P(),
        P(),
        P(),
        P(),
        P(),
        P(),
        P(),
        P(rows, None),
        P(rows),
    )
    return jax.shard_map(
        on_device,
        mesh=grid,
        in_specs=in_specs,
        out_specs=P(rows, "head", None, None),
        check_vma=False,
    )
```

```python
import functools

import jax
import jax.numpy as jnp
from jax import lax
from jax.experimental import pallas as pl
from jax.experimental.pallas import tpu as pltpu
from jax.sharding import Mesh, PartitionSpec as P

D = 1024
HEADS = 16
HD = 64
CH = 256
SLOTS = 26
STRIP = 64
NEG = -2e38
bf16 = jnp.bfloat16
f32 = jnp.float32


def split(v):
    hi = v.astype(bf16)
    return hi, (v - hi.astype(f32)).astype(bf16)


def dot(a, b):
    return jnp.dot(a, b, preferred_element_type=f32)


def dot3(ah, al, bh, bl):
    m = ah.shape[0]
    both = dot(jnp.concatenate([ah, al], axis=0), bh)
    return both[:m] + (both[m:] + dot(ah, bl))


def lanes(shape):
    return lax.broadcasted_iota(jnp.int32, shape, len(shape) - 1)


def qkv_body(x_ref, w_ref, out_ref, xh, xl):
    @pl.when(pl.program_id(0) == 0)
    def _():
        hi, lo = split(x_ref[...])
        xh[...] = hi
        xl[...] = lo

    wh, wl = split(w_ref[...])
    r = dot3(xh[...], xl[...], wh, wl)
    for u in range(2):
        q = r[:, u * 192 : u * 192 + HD] * 0.125
        k = r[:, u * 192 + HD : u * 192 + 2 * HD]
        v = r[:, u * 192 + 2 * HD : u * 192 + 3 * HD]
        for i, t in enumerate((q, k)):
            lo = t - t.astype(bf16).astype(f32)
            out_ref[u, i * 128 : i * 128 + 128, :] = jnp.concatenate([t, lo], axis=1).astype(bf16)
        out_ref[u, 256:320, :] = jnp.concatenate([v[:STRIP], v[STRIP:]], axis=1).astype(bf16)


def qkv(x, w):
    return pl.pallas_call(
        qkv_body,
        grid=(HEADS // 2,),
        in_specs=[
            pl.BlockSpec((128, D), lambda g: (0, 0)),
            pl.BlockSpec((D, 384), lambda g: (0, g)),
        ],
        out_specs=pl.BlockSpec((2, 320, 128), lambda g: (g, 0, 0)),
        out_shape=jax.ShapeDtypeStruct((HEADS, 320, 128), bf16),
        scratch_shapes=[pltpu.VMEM((128, D), bf16), pltpu.VMEM((128, D), bf16)],
        name="qkv",
    )(x, w)


UNROLL = 8
PAIRS = 16 * (SLOTS // 2)
ROOM = PAIRS + UNROLL


def attend_body(sets, items, cnt, info, kv0, kv1, *refs):
    qrefs, (o_ref, ks, vs, qs, sc, ms, accs) = refs[:-7], refs[-7:]
    low = lanes((128, 128)) < HD

    def strips(ref, j, rows):
        return jnp.concatenate([ref[2 * j, rows, :], ref[2 * j + 1, rows, :]], axis=0)

    def ready(j, _):
        for fr in range(2):
            rows = slice(fr * 64, fr * 64 + 64)
            for src, kv in enumerate((kv0, kv1)):
                b = src * 16 + fr * 8 + j
                a = strips(kv, j, rows).astype(f32)
                swapped = pltpu.roll(a, 64, 1)
                ks[b, :, 0:128] = jnp.where(low, a, swapped).astype(bf16)
                ks[b, :, 128:256] = swapped.astype(bf16)
                v = strips(kv, j, slice(128, 192)).astype(f32)
                if fr:
                    v = pltpu.roll(v, 64, 1)
                vs[b] = jnp.where(low, v, 1.0).astype(bf16)
        return 0

    lax.fori_loop(0, 8, ready, 0)

    for i in range(len(sets)):
        mine = (qrefs[i],) if len(sets) > 1 else qrefs
        for part, q in enumerate(mine):

            def ready_q(j, _, i=i, part=part, q=q):
                for fr in range(2):
                    rows = slice(fr * 64, fr * 64 + 64)
                    qs[17 * i + fr * 8 + 4 * part + j] = strips(q, j, rows)
                return 0

            lax.fori_loop(0, 8 // len(mine), ready_q, 0)
        qs[17 * i + 16] = jnp.zeros((128, 128), bf16)
    vs[32] = jnp.zeros((128, 128), bf16)
    eye = lax.broadcasted_iota(jnp.int32, (128, 128), 0) == lanes((128, 128))

    def clear(b, _):
        ms[b] = jnp.full((128, 128), NEG, f32)
        return 0

    lax.fori_loop(0, 17, clear, 0)
    accs[16] = jnp.zeros((128, 128), f32)

    def one_set(i, _):
        s = sets[0]
        for n in range(1, len(sets)):
            s = jnp.where(i == n, sets[n], s)
        trips = (cnt[s] + UNROLL - 1) // UNROLL

        def score(t, _):
            got = []
            for u in range(UNROLL):
                item = items[s, t * UNROLL + u]
                ia = (item >> 6) & 31
                ib = item & 63
                a = qs[17 * i + (item >> 11)]
                got.append(
                    lax.dot_general(
                        jnp.concatenate([a, a[:, :HD]], axis=1),
                        jnp.concatenate(
                            [ks[ia, :, :192], ks[jnp.where(ib == 32, ia, ib), :, :192]], axis=0
                        ),
                        (((1,), (1,)), ((), ())),
                        preferred_element_type=f32,
                    )
                )
            for u in range(UNROLL):
                qi = items[s, t * UNROLL + u] >> 11
                sc[t * UNROLL + u] = got[u]
                ms[qi] = jnp.maximum(ms[qi], jnp.maximum(got[u][:, :128], got[u][:, 128:]))
            return 0

        lax.fori_loop(0, trips, score, 0)

        def peak(b, _):
            for u in range(8):
                m = jnp.max(ms[8 * b + u], axis=1, keepdims=True)
                ms[8 * b + u] = jnp.broadcast_to(m, (128, 128))
                accs[8 * b + u] = jnp.zeros((128, 128), f32)
            return 0

        lax.fori_loop(0, 2, peak, 0)

        def blend(t, _):
            got = []
            for u in range(UNROLL):
                item = items[s, t * UNROLL + u]
                m = ms[item >> 11]
                p = jnp.exp(sc[t * UNROLL + u] - jnp.concatenate([m, m], axis=1))
                v = jnp.concatenate([vs[(item >> 6) & 31], vs[item & 63]], axis=0)
                got.append(dot(p.astype(bf16), v))
            for u in range(UNROLL):
                qi = items[s, t * UNROLL + u] >> 11
                accs[qi] = accs[qi] + got[u]
            return 0

        lax.fori_loop(0, trips, blend, 0)
        to = info[s] if len(sets) > 1 else 0

        def diagonal(v):
            return jnp.sum(jnp.where(eye, v, 0.0), axis=0, keepdims=True)

        def emit(jj, _):
            emit_one(2 * jj)
            emit_one(2 * jj + 1)
            return 0

        def emit_one(j):
            a0 = accs[j]
            a1 = accs[8 + j]
            s0 = pltpu.roll(a0, 64, 1)
            s1 = pltpu.roll(a1, 64, 1)
            total = jnp.maximum(jnp.where(low, s0, a1), 0.5)
            out = (jnp.where(low, a0, s1) / total).astype(bf16)
            l0 = jnp.maximum(diagonal(jnp.where(low, s0, a0)), 0.5)
            l1 = jnp.maximum(diagonal(jnp.where(low, s1, a1)), 0.5)
            t0 = diagonal(ms[j]) + jnp.log(l0)
            t1 = diagonal(ms[8 + j]) + jnp.log(l1)
            ms[j] = jnp.full((128, 128), NEG, f32)
            ms[8 + j] = jnp.full((128, 128), NEG, f32)
            sub = lax.broadcasted_iota(jnp.int32, (8, 128), 0)
            for half in range(2):
                o_ref[to, 2 * j + half, 0:64, :] = out[half * 64 : half * 64 + 64]
                c = half * 64
                row = jnp.concatenate([t0[:, c : c + 64], t1[:, c : c + 64]], axis=1)
                hi = row.astype(bf16).astype(f32)
                mid = (row - hi).astype(bf16).astype(f32)
                last = row - hi - mid
                tile = jnp.where(
                    sub == 0, hi, jnp.where(sub == 1, mid, jnp.where(sub == 2, last, 0.0))
                )
                o_ref[to, 2 * j + half, 64:72, :] = tile.astype(bf16)

        lax.fori_loop(0, 4, emit, 0)
        return 0

    lax.fori_loop(0, len(sets), one_set, 0)


def attend(sets, items, cnt, info, kv0, kv1, qs):
    smem = pl.BlockSpec(memory_space=pltpu.SMEM)
    vmem = pl.BlockSpec(memory_space=pltpu.VMEM)
    return pl.pallas_call(
        functools.partial(attend_body, sets),
        in_specs=[smem, smem, smem] + [vmem] * (2 + len(qs)),
        out_specs=vmem,
        out_shape=jax.ShapeDtypeStruct((4 if len(sets) > 1 else 1, HEADS, 72, 128), bf16),
        scratch_shapes=[
            pltpu.VMEM((32, 128, 256), bf16),
            pltpu.VMEM((33, 128, 128), bf16),
            pltpu.VMEM((17 * len(sets), 128, 128), bf16),
            pltpu.VMEM((ROOM, 128, 256), f32),
            pltpu.VMEM((17, 128, 128), f32),
            pltpu.VMEM((17, 128, 128), f32),
        ],
        compiler_params=pltpu.CompilerParams(vmem_limit_bytes=38 << 20),
    )(items, cnt, info, kv0, kv1, *qs)


def mix_body(r_ref, x_ref, w_ref, gain_ref, proj_ref, feat_ref, top_ref, bot_ref, att):
    lse = jnp.sum(r_ref[:, 64:72, :].astype(f32), axis=1)
    parts = [lse[16 * x : 16 * x + 16] for x in range(4)]
    peak = jnp.maximum(jnp.maximum(parts[0], parts[1]), jnp.maximum(parts[2], parts[3]))
    es = [jnp.exp(p - peak) for p in parts]
    total = (es[0] + es[1]) + (es[2] + es[3])
    share = jnp.concatenate([e / total for e in es], axis=0)
    share = jnp.concatenate([share, share], axis=0).T
    both = jnp.where(lanes((STRIP, 128)) < 64, share[:STRIP], share[STRIP:])
    bh, bl = split(both)
    low = lanes((STRIP, 128)) < HD
    row = lax.broadcasted_iota(jnp.int32, (128, 2048), 0)
    col = lanes((128, 2048))
    half = (row >= 64) == (col % 128 >= 64)
    wide = []
    for x in range(4):
        spread = jnp.where(half & (row % 64 == 16 * x + col // 128), 1.0, 0.0).astype(bf16)
        wide.append(dot(bh, spread) + dot(bl, spread))
    for p in range(HEADS // 2):
        t = []
        for h in (2 * p, 2 * p + 1):
            acc = None
            for x in range(4):
                o = r_ref[16 * x + h, 0:64, :].astype(f32) * wide[x][:, 128 * h : 128 * h + 128]
                acc = o if acc is None else acc + o
            t.append(acc)
        att[0:64, 128 * p : 128 * p + 128] = jnp.where(low, t[0], pltpu.roll(t[1], 64, 1))
        att[64:128, 128 * p : 128 * p + 128] = jnp.where(low, pltpu.roll(t[0], 64, 1), t[1])
    ah, al = split(att[...])
    wh, wl = split(w_ref[...])
    stream = x_ref[...] + dot3(ah, al, wh, wl)
    centred = stream - jnp.mean(stream, axis=1, keepdims=True)
    spread = jnp.mean(centred * centred, axis=1, keepdims=True)
    normed = centred * lax.rsqrt(spread + 1e-05) * gain_ref[...]
    nh, nl = split(normed)
    ph, plo = split(proj_ref[...])
    feat = dot3(nh, nl, ph, plo).astype(bf16)
    feat_ref[...] = feat
    for f in range(2):
        top_ref[32 * f : 32 * f + 32] = feat[64 * f : 64 * f + 32]
        bot_ref[32 * f : 32 * f + 32] = feat[64 * f + 32 : 64 * f + 64]


def mix(r, x, w, gain, proj):
    return pl.pallas_call(
        mix_body,
        out_shape=(
            jax.ShapeDtypeStruct((128, CH), bf16),
            jax.ShapeDtypeStruct((64, CH), bf16),
            jax.ShapeDtypeStruct((64, CH), bf16),
        ),
        scratch_shapes=[pltpu.VMEM((128, D), f32)],
        compiler_params=pltpu.CompilerParams(vmem_limit_bytes=20 << 20),
        name="mix",
    )(r, x, w, gain, proj)


def shifted(dst, src, rows, relu):
    def one(r, _):
        for dx in range(3):
            for half in range(2):
                v = src[half * rows + r, pl.ds(7 + dx, 128), :]
                if relu:
                    v = jnp.maximum(v, 0.0)
                dst[r, :, dx * 256 + half * 128 : dx * 256 + half * 128 + 128] = v.astype(bf16)
        return 0

    lax.fori_loop(0, rows, one, 0)


def head_body(pos, feat_ref, above_ref, below_ref, up_ref, cw_ref, cb_ref, out_ref, ups, u3, hid, h3):
    at = pos[0]

    @pl.when(pl.program_id(0) == 0)
    def _():
        for ref, rows in ((ups, 24), (hid, 20)):
            ref[:, 0:8, :] = jnp.zeros((rows, 8, 128), f32)
            ref[:, 136:144, :] = jnp.zeros((rows, 8, 128), f32)

    own = feat_ref[...]
    early = jnp.concatenate([own, below_ref[...]], axis=0)
    late = jnp.concatenate([above_ref[...], own], axis=0)
    for a in range(4):
        src = early if a < 2 else late
        lifted = dot(src, up_ref[:, 1024 * a : 1024 * a + 1024]).astype(bf16).astype(f32)
        for i in range(3):
            row = 2 + 4 * i + a if a < 2 else 4 * i + a - 2
            for e in range(4):
                for half in range(2):
                    c = 256 * e + 128 * half
                    ups[12 * half + row, pl.ds(8 + e, 32, stride=4), :] = lifted[
                        32 * i : 32 * i + 32, c : c + 128
                    ]
    shifted(u3, ups, 12, True)

    def conv1(r, _):
        acc = None
        for dy in range(3):
            part = dot(u3[pl.ds(2 * r + dy, 2)].reshape(256, 768), cw_ref[0, dy])
            acc = part if acc is None else acc + part
        h = jnp.maximum(acc + cb_ref[0:1, :], 0.0).astype(bf16).astype(f32)
        for k in range(2):
            y = 2 * r + k
            keep = ((y > 0) | (at > 0)) & ((y < 9) | (at < 15))
            v = jnp.where(keep, h[128 * k : 128 * k + 128], 0.0)
            for half in range(2):
                hid[10 * half + y, 8:136, :] = v[:, 128 * half : 128 * half + 128]
        return 0

    lax.fori_loop(0, 5, conv1, 0)
    shifted(h3, hid, 10, False)

    def conv2(r, _):
        acc = None
        for dy in range(3):
            part = dot(h3[pl.ds(2 * r + dy, 2)].reshape(256, 768), cw_ref[1, dy])
            acc = part if acc is None else acc + part
        acc = acc + cb_ref[1:2, :]
        for k in range(2):
            y = 2 * r + k
            for half in range(2):
                c = 128 * half
                v = ups[12 * half + y + 2, 8:136, :] + acc[128 * k : 128 * k + 128, c : c + 128]
                out_ref[0, y, :, c : c + 128] = v.astype(bf16)
        return 0

    lax.fori_loop(0, 4, conv2, 0)


def dense_head(pos, feat, above, below, up, cw, cb):
    whole = lambda shape: pl.BlockSpec(shape, lambda f: (0,) * len(shape))
    return pl.pallas_call(
        head_body,
        grid=(2,),
        in_specs=[
            pl.BlockSpec(memory_space=pltpu.SMEM),
            pl.BlockSpec((64, CH), lambda f: (f, 0)),
            pl.BlockSpec((32, CH), lambda f: (f, 0)),
            pl.BlockSpec((32, CH), lambda f: (f, 0)),
            whole((CH, 16 * CH)),
            whole((2, 3, 3 * CH, CH)),
            whole((2, CH)),
        ],
        out_specs=pl.BlockSpec((1, 8, 128, CH), lambda f: (f, 0, 0, 0)),
        out_shape=jax.ShapeDtypeStruct((2, 8, 128, CH), bf16),
        scratch_shapes=[
            pltpu.VMEM((24, 144, 128), f32),
            pltpu.VMEM((12, 128, 768), bf16),
            pltpu.VMEM((20, 144, 128), f32),
            pltpu.VMEM((10, 128, 768), bf16),
        ],
        compiler_params=pltpu.CompilerParams(vmem_limit_bytes=24 << 20),
        name="dense_head",
    )(pos, feat, above, below, up, cw, cb)


def local_items(lists, counts, x, z):
    packed = jnp.concatenate([lists, counts[:, None]], axis=1)
    sets = [packed] + [
        lax.ppermute(packed, "x", [(i, (i + k) % 4) for i in range(4)]) for k in (1, 2, 3)
    ]
    packed = jnp.stack(sets, axis=0)
    ids = packed[:, :, :SLOTS]
    slot = jnp.arange(SLOTS, dtype=jnp.int32)
    block = jnp.arange(16, dtype=jnp.int32)
    mine = (slot < packed[:, :, SLOTS:]) & ((ids // 16) % 4 == x)
    local = jnp.where(ids // 64 == z, 0, 16) + ids % 16
    ones = mine.astype(jnp.int32)
    inside = jnp.sum(jnp.where(slot[None, :] < slot[:, None], ones[:, :, None, :], 0), axis=-1)
    total = jnp.sum(ones, axis=-1)
    pairs = (total + 1) // 2
    ahead = jnp.sum(jnp.where(block[None, :] < block[:, None], pairs[:, None, :], 0), axis=-1)
    place = jnp.where(mine, ahead[:, :, None] + inside // 2, -1).reshape(4, 1, -1)
    alone = jnp.where(inside + 1 == total[:, :, None], 32, 0)
    value = jnp.where(inside % 2 == 0, block[:, None] * 2048 + local * 64 + alone, local)
    at = jnp.arange(ROOM, dtype=jnp.int32)[:, None]
    items = jnp.sum(jnp.where(place == at, value.reshape(4, 1, -1), 0), axis=-1)
    count = jnp.sum(pairs, axis=-1)
    items = jnp.where(at[:, 0] < count[:, None], items, 16 * 2048 + 32)
    return items, count


def on_device(tokens, qkv_w, out_w, gain, proj_w, up_w, conv_w, conv_b, lists, counts):
    x = lax.axis_index("x")
    z = lax.axis_index("z")
    strip = lax.axis_index("head")
    flat = tokens.reshape(-1, D)
    right = [(i, (i + 1) % 4) for i in range(4)]
    left = [(i, (i - 1) % 4) for i in range(4)]
    packed = qkv(flat, qkv_w)
    packed, lists, counts = lax.optimization_barrier((packed, lists, counts))
    items, cnt = local_items(lists, counts, x, z)
    packed = lax.all_to_all(packed, "head", split_axis=0, concat_axis=0, tiled=True)
    q = packed[:, :128]
    kv = packed[:, 128:]
    kv_far = lax.ppermute(kv, "z", [(0, 1), (1, 0)])
    q1 = lax.ppermute(q, "x", right)
    q3 = lax.ppermute(q, "x", left)
    q2a = lax.ppermute(q1[:8], "x", right)
    q2b = lax.ppermute(q3[8:], "x", left)
    info = (x - jnp.arange(4, dtype=jnp.int32)) % 4
    part = attend((0, 1, 3), items, cnt, info, kv, kv_far, [q, q1, q3])
    last = attend((2,), items, cnt, info, kv, kv_far, [q2a, q2b])
    part = lax.dynamic_update_slice_in_dim(part, last, info[2], 0)
    part = lax.all_to_all(
        part.reshape(64, 72, 128), ("x", "head"), split_axis=0, concat_axis=0, tiled=True
    )
    feat, top, bot = mix(part, flat, out_w, gain[None, :], proj_w)
    above = lax.ppermute(bot, "head", [(i, i + 1) for i in range(15)])
    below = lax.ppermute(top, "head", [(i + 1, i) for i in range(15)])
    return dense_head(
        strip[None], feat, above, below, up_w, conv_w.reshape(2, 3, 3 * CH, CH), conv_b
    )


def solution(mesh):
    grid = Mesh(mesh.devices.reshape(2, 4, 16), ("z", "x", "head"))
    rows = ("z", "x")
    in_specs = (
        P(rows, "head", None),
        P(),
        P(),
        P(),
        P(),
        P(),
        P(),
        P(),
        P(rows, None),
        P(rows),
    )
    return jax.shard_map(
        on_device,
        mesh=grid,
        in_specs=in_specs,
        out_specs=P(rows, "head", None, None),
        check_vma=False,
    )
```

```python
import functools

import jax
import jax.numpy as jnp
from jax import lax
from jax.experimental import pallas as pl
from jax.experimental.pallas import tpu as pltpu
from jax.sharding import Mesh, PartitionSpec as P

D = 1024
HEADS = 16
HD = 64
CH = 256
SLOTS = 26
STRIP = 64
NEG = -2e38
bf16 = jnp.bfloat16
f32 = jnp.float32


def split(v):
    hi = v.astype(bf16)
    return hi, (v - hi.astype(f32)).astype(bf16)


def dot(a, b):
    return jnp.dot(a, b, preferred_element_type=f32)


def dot3(ah, al, bh, bl):
    m = ah.shape[0]
    both = dot(jnp.concatenate([ah, al], axis=0), bh)
    return both[:m] + (both[m:] + dot(ah, bl))


def lanes(shape):
    return lax.broadcasted_iota(jnp.int32, shape, len(shape) - 1)


def qkv_body(x_ref, w_ref, out_ref, xh, xl):
    @pl.when(pl.program_id(0) == 0)
    def _():
        hi, lo = split(x_ref[...])
        xh[...] = hi
        xl[...] = lo

    wh, wl = split(w_ref[...])
    r = dot3(xh[...], xl[...], wh, wl)
    for u in range(4):
        q = r[:, u * 192 : u * 192 + HD] * 0.125
        k = r[:, u * 192 + HD : u * 192 + 2 * HD]
        v = r[:, u * 192 + 2 * HD : u * 192 + 3 * HD]
        for i, t in enumerate((q, k)):
            lo = t - t.astype(bf16).astype(f32)
            out_ref[u, i * 128 : i * 128 + 128, :] = jnp.concatenate([t, lo], axis=1).astype(bf16)
        out_ref[u, 256:320, :] = jnp.concatenate([v[:STRIP], v[STRIP:]], axis=1).astype(bf16)


def qkv(x, w):
    return pl.pallas_call(
        qkv_body,
        grid=(HEADS // 4,),
        in_specs=[
            pl.BlockSpec((128, D), lambda g: (0, 0)),
            pl.BlockSpec((D, 768), lambda g: (0, g)),
        ],
        out_specs=pl.BlockSpec((4, 320, 128), lambda g: (g, 0, 0)),
        out_shape=jax.ShapeDtypeStruct((HEADS, 320, 128), bf16),
        scratch_shapes=[pltpu.VMEM((128, D), bf16), pltpu.VMEM((128, D), bf16)],
        name="qkv",
    )(x, w)


UNROLL = 8
PAIRS = 16 * (SLOTS // 2)
ROOM = PAIRS + UNROLL


def attend_body(sets, items, cnt, info, kv0, kv1, *refs):
    qrefs, (o_ref, ks, vs, qs, sc, ms, accs) = refs[:-7], refs[-7:]
    low = lanes((128, 128)) < HD

    def strips(ref, j, rows):
        return jnp.concatenate([ref[2 * j, rows, :], ref[2 * j + 1, rows, :]], axis=0)

    def ready(j, _):
        for fr in range(2):
            rows = slice(fr * 64, fr * 64 + 64)
            for src, kv in enumerate((kv0, kv1)):
                b = src * 16 + fr * 8 + j
                a = strips(kv, j, rows).astype(f32)
                swapped = pltpu.roll(a, 64, 1)
                ks[b, :, 0:128] = jnp.where(low, a, swapped).astype(bf16)
                ks[b, :, 128:256] = swapped.astype(bf16)
                v = strips(kv, j, slice(128, 192)).astype(f32)
                if fr:
                    v = pltpu.roll(v, 64, 1)
                vs[b] = jnp.where(low, v, 1.0).astype(bf16)
        return 0

    lax.fori_loop(0, 8, ready, 0)

    for i in range(len(sets)):
        mine = (qrefs[i],) if len(sets) > 1 else qrefs
        for part, q in enumerate(mine):

            def ready_q(j, _, i=i, part=part, q=q):
                for fr in range(2):
                    rows = slice(fr * 64, fr * 64 + 64)
                    qs[17 * i + fr * 8 + 4 * part + j] = strips(q, j, rows)
                return 0

            lax.fori_loop(0, 8 // len(mine), ready_q, 0)
        qs[17 * i + 16] = jnp.zeros((128, 128), bf16)
    vs[32] = jnp.zeros((128, 128), bf16)
    eye = lax.broadcasted_iota(jnp.int32, (128, 128), 0) == lanes((128, 128))

    def clear(b, _):
        ms[b] = jnp.full((128, 128), NEG, f32)
        return 0

    lax.fori_loop(0, 17, clear, 0)
    accs[16] = jnp.zeros((128, 128), f32)

    def one_set(i, _):
        s = sets[0]
        for n in range(1, len(sets)):
            s = jnp.where(i == n, sets[n], s)
        trips = (cnt[s] + UNROLL - 1) // UNROLL

        def score(t, _):
            got = []
            for u in range(UNROLL):
                item = items[s, t * UNROLL + u]
                ia = (item >> 6) & 31
                ib = item & 63
                a = qs[17 * i + (item >> 11)]
                got.append(
                    lax.dot_general(
                        jnp.concatenate([a, a[:, :HD]], axis=1),
                        jnp.concatenate(
                            [ks[ia, :, :192], ks[jnp.where(ib == 32, ia, ib), :, :192]], axis=0
                        ),
                        (((1,), (1,)), ((), ())),
                        preferred_element_type=f32,
                    )
                )
            for u in range(UNROLL):
                qi = items[s, t * UNROLL + u] >> 11
                sc[t * UNROLL + u] = got[u]
                ms[qi] = jnp.maximum(ms[qi], jnp.maximum(got[u][:, :128], got[u][:, 128:]))
            return 0

        lax.fori_loop(0, trips, score, 0)

        def peak(b, _):
            for u in range(8):
                m = jnp.max(ms[8 * b + u], axis=1, keepdims=True)
                ms[8 * b + u] = jnp.broadcast_to(m, (128, 128))
                accs[8 * b + u] = jnp.zeros((128, 128), f32)
            return 0

        lax.fori_loop(0, 2, peak, 0)

        def blend(t, _):
            got = []
            for u in range(UNROLL):
                item = items[s, t * UNROLL + u]
                m = ms[item >> 11]
                p = jnp.exp(sc[t * UNROLL + u] - jnp.concatenate([m, m], axis=1))
                v = jnp.concatenate([vs[(item >> 6) & 31], vs[item & 63]], axis=0)
                got.append(dot(p.astype(bf16), v))
            for u in range(UNROLL):
                qi = items[s, t * UNROLL + u] >> 11
                accs[qi] = accs[qi] + got[u]
            return 0

        lax.fori_loop(0, trips, blend, 0)
        to = info[s] if len(sets) > 1 else 0

        def diagonal(v):
            return jnp.sum(jnp.where(eye, v, 0.0), axis=0, keepdims=True)

        def emit(jj, _):
            emit_one(2 * jj)
            emit_one(2 * jj + 1)
            return 0

        def emit_one(j):
            a0 = accs[j]
            a1 = accs[8 + j]
            s0 = pltpu.roll(a0, 64, 1)
            s1 = pltpu.roll(a1, 64, 1)
            total = jnp.maximum(jnp.where(low, s0, a1), 0.5)
            out = (jnp.where(low, a0, s1) / total).astype(bf16)
            l0 = jnp.maximum(diagonal(jnp.where(low, s0, a0)), 0.5)
            l1 = jnp.maximum(diagonal(jnp.where(low, s1, a1)), 0.5)
            t0 = diagonal(ms[j]) + jnp.log(l0)
            t1 = diagonal(ms[8 + j]) + jnp.log(l1)
            ms[j] = jnp.full((128, 128), NEG, f32)
            ms[8 + j] = jnp.full((128, 128), NEG, f32)
            sub = lax.broadcasted_iota(jnp.int32, (8, 128), 0)
            for half in range(2):
                o_ref[to, 2 * j + half, 0:64, :] = out[half * 64 : half * 64 + 64]
                c = half * 64
                row = jnp.concatenate([t0[:, c : c + 64], t1[:, c : c + 64]], axis=1)
                hi = row.astype(bf16).astype(f32)
                mid = (row - hi).astype(bf16).astype(f32)
                last = row - hi - mid
                tile = jnp.where(
                    sub == 0, hi, jnp.where(sub == 1, mid, jnp.where(sub == 2, last, 0.0))
                )
                o_ref[to, 2 * j + half, 64:72, :] = tile.astype(bf16)

        lax.fori_loop(0, 4, emit, 0)
        return 0

    lax.fori_loop(0, len(sets), one_set, 0)


def attend(sets, items, cnt, info, kv0, kv1, qs):
    smem = pl.BlockSpec(memory_space=pltpu.SMEM)
    vmem = pl.BlockSpec(memory_space=pltpu.VMEM)
    return pl.pallas_call(
        functools.partial(attend_body, sets),
        in_specs=[smem, smem, smem] + [vmem] * (2 + len(qs)),
        out_specs=vmem,
        out_shape=jax.ShapeDtypeStruct((4 if len(sets) > 1 else 1, HEADS, 72, 128), bf16),
        scratch_shapes=[
            pltpu.VMEM((32, 128, 256), bf16),
            pltpu.VMEM((33, 128, 128), bf16),
            pltpu.VMEM((17 * len(sets), 128, 128), bf16),
            pltpu.VMEM((ROOM, 128, 256), f32),
            pltpu.VMEM((17, 128, 128), f32),
            pltpu.VMEM((17, 128, 128), f32),
        ],
        compiler_params=pltpu.CompilerParams(vmem_limit_bytes=38 << 20),
    )(items, cnt, info, kv0, kv1, *qs)


def mix_body(r_ref, x_ref, w_ref, gain_ref, proj_ref, feat_ref, top_ref, bot_ref, att):
    lse = jnp.sum(r_ref[:, 64:72, :].astype(f32), axis=1)
    parts = [lse[16 * x : 16 * x + 16] for x in range(4)]
    peak = jnp.maximum(jnp.maximum(parts[0], parts[1]), jnp.maximum(parts[2], parts[3]))
    es = [jnp.exp(p - peak) for p in parts]
    total = (es[0] + es[1]) + (es[2] + es[3])
    share = jnp.concatenate([e / total for e in es], axis=0)
    share = jnp.concatenate([share, share], axis=0).T
    both = jnp.where(lanes((STRIP, 128)) < 64, share[:STRIP], share[STRIP:])
    bh, bl = split(both)
    low = lanes((STRIP, 128)) < HD
    row = lax.broadcasted_iota(jnp.int32, (128, 2048), 0)
    col = lanes((128, 2048))
    half = (row >= 64) == (col % 128 >= 64)
    wide = []
    for x in range(4):
        spread = jnp.where(half & (row % 64 == 16 * x + col // 128), 1.0, 0.0).astype(bf16)
        wide.append(dot(bh, spread) + dot(bl, spread))
    for p in range(HEADS // 2):
        t = []
        for h in (2 * p, 2 * p + 1):
            acc = None
            for x in range(4):
                o = r_ref[16 * x + h, 0:64, :].astype(f32) * wide[x][:, 128 * h : 128 * h + 128]
                acc = o if acc is None else acc + o
            t.append(acc)
        att[0:64, 128 * p : 128 * p + 128] = jnp.where(low, t[0], pltpu.roll(t[1], 64, 1))
        att[64:128, 128 * p : 128 * p + 128] = jnp.where(low, pltpu.roll(t[0], 64, 1), t[1])
    ah, al = split(att[...])
    wh, wl = split(w_ref[...])
    stream = x_ref[...] + dot3(ah, al, wh, wl)
    centred = stream - jnp.mean(stream, axis=1, keepdims=True)
    spread = jnp.mean(centred * centred, axis=1, keepdims=True)
    normed = centred * lax.rsqrt(spread + 1e-05) * gain_ref[...]
    nh, nl = split(normed)
    ph, plo = split(proj_ref[...])
    feat = dot3(nh, nl, ph, plo).astype(bf16)
    feat_ref[...] = feat
    for f in range(2):
        top_ref[32 * f : 32 * f + 32] = feat[64 * f : 64 * f + 32]
        bot_ref[32 * f : 32 * f + 32] = feat[64 * f + 32 : 64 * f + 64]


def mix(r, x, w, gain, proj):
    return pl.pallas_call(
        mix_body,
        out_shape=(
            jax.ShapeDtypeStruct((128, CH), bf16),
            jax.ShapeDtypeStruct((64, CH), bf16),
            jax.ShapeDtypeStruct((64, CH), bf16),
        ),
        scratch_shapes=[pltpu.VMEM((128, D), f32)],
        compiler_params=pltpu.CompilerParams(vmem_limit_bytes=20 << 20),
        name="mix",
    )(r, x, w, gain, proj)


def shifted(dst, src, rows, relu):
    def one(r, _):
        for dx in range(3):
            for half in range(2):
                v = src[half * rows + r, pl.ds(7 + dx, 128), :]
                if relu:
                    v = jnp.maximum(v, 0.0)
                dst[r, :, dx * 256 + half * 128 : dx * 256 + half * 128 + 128] = v.astype(bf16)
        return 0

    lax.fori_loop(0, rows, one, 0)


def head_body(pos, feat_ref, above_ref, below_ref, up_ref, cw_ref, cb_ref, out_ref, ups, u3, hid, h3):
    at = pos[0]

    @pl.when(pl.program_id(0) == 0)
    def _():
        for ref, rows in ((ups, 24), (hid, 20)):
            ref[:, 0:8, :] = jnp.zeros((rows, 8, 128), f32)
            ref[:, 136:144, :] = jnp.zeros((rows, 8, 128), f32)

    own = feat_ref[...]
    early = jnp.concatenate([own, below_ref[...]], axis=0)
    late = jnp.concatenate([above_ref[...], own], axis=0)
    for a in range(4):
        src = early if a < 2 else late
        lifted = dot(src, up_ref[:, 1024 * a : 1024 * a + 1024]).astype(bf16).astype(f32)
        for i in range(3):
            row = 2 + 4 * i + a if a < 2 else 4 * i + a - 2
            for e in range(4):
                for half in range(2):
                    c = 256 * e + 128 * half
                    ups[12 * half + row, pl.ds(8 + e, 32, stride=4), :] = lifted[
                        32 * i : 32 * i + 32, c : c + 128
                    ]
    shifted(u3, ups, 12, True)

    def conv1(r, _):
        acc = None
        for dy in range(3):
            part = dot(u3[pl.ds(2 * r + dy, 2)].reshape(256, 768), cw_ref[0, dy])
            acc = part if acc is None else acc + part
        h = jnp.maximum(acc + cb_ref[0:1, :], 0.0).astype(bf16).astype(f32)
        for k in range(2):
            y = 2 * r + k
            keep = ((y > 0) | (at > 0)) & ((y < 9) | (at < 15))
            v = jnp.where(keep, h[128 * k : 128 * k + 128], 0.0)
            for half in range(2):
                hid[10 * half + y, 8:136, :] = v[:, 128 * half : 128 * half + 128]
        return 0

    lax.fori_loop(0, 5, conv1, 0)
    shifted(h3, hid, 10, False)

    def conv2(r, _):
        acc = None
        for dy in range(3):
            part = dot(h3[pl.ds(2 * r + dy, 2)].reshape(256, 768), cw_ref[1, dy])
            acc = part if acc is None else acc + part
        acc = acc + cb_ref[1:2, :]
        for k in range(2):
            y = 2 * r + k
            for half in range(2):
                c = 128 * half
                v = ups[12 * half + y + 2, 8:136, :] + acc[128 * k : 128 * k + 128, c : c + 128]
                out_ref[0, y, :, c : c + 128] = v.astype(bf16)
        return 0

    lax.fori_loop(0, 4, conv2, 0)


def dense_head(pos, feat, above, below, up, cw, cb):
    whole = lambda shape: pl.BlockSpec(shape, lambda f: (0,) * len(shape))
    return pl.pallas_call(
        head_body,
        grid=(2,),
        in_specs=[
            pl.BlockSpec(memory_space=pltpu.SMEM),
            pl.BlockSpec((64, CH), lambda f: (f, 0)),
            pl.BlockSpec((32, CH), lambda f: (f, 0)),
            pl.BlockSpec((32, CH), lambda f: (f, 0)),
            whole((CH, 16 * CH)),
            whole((2, 3, 3 * CH, CH)),
            whole((2, CH)),
        ],
        out_specs=pl.BlockSpec((1, 8, 128, CH), lambda f: (f, 0, 0, 0)),
        out_shape=jax.ShapeDtypeStruct((2, 8, 128, CH), bf16),
        scratch_shapes=[
            pltpu.VMEM((24, 144, 128), f32),
            pltpu.VMEM((12, 128, 768), bf16),
            pltpu.VMEM((20, 144, 128), f32),
            pltpu.VMEM((10, 128, 768), bf16),
        ],
        compiler_params=pltpu.CompilerParams(vmem_limit_bytes=24 << 20),
        name="dense_head",
    )(pos, feat, above, below, up, cw, cb)


def local_items(lists, counts, x, z):
    packed = jnp.concatenate([lists, counts[:, None]], axis=1)
    sets = [packed] + [
        lax.ppermute(packed, "x", [(i, (i + k) % 4) for i in range(4)]) for k in (1, 2, 3)
    ]
    packed = jnp.stack(sets, axis=0)
    ids = packed[:, :, :SLOTS]
    slot = jnp.arange(SLOTS, dtype=jnp.int32)
    block = jnp.arange(16, dtype=jnp.int32)
    mine = (slot < packed[:, :, SLOTS:]) & ((ids // 16) % 4 == x)
    local = jnp.where(ids // 64 == z, 0, 16) + ids % 16
    ones = mine.astype(jnp.int32)
    inside = jnp.sum(jnp.where(slot[None, :] < slot[:, None], ones[:, :, None, :], 0), axis=-1)
    total = jnp.sum(ones, axis=-1)
    pairs = (total + 1) // 2
    ahead = jnp.sum(jnp.where(block[None, :] < block[:, None], pairs[:, None, :], 0), axis=-1)
    place = jnp.where(mine, ahead[:, :, None] + inside // 2, -1).reshape(4, 1, -1)
    alone = jnp.where(inside + 1 == total[:, :, None], 32, 0)
    value = jnp.where(inside % 2 == 0, block[:, None] * 2048 + local * 64 + alone, local)
    at = jnp.arange(ROOM, dtype=jnp.int32)[:, None]
    items = jnp.sum(jnp.where(place == at, value.reshape(4, 1, -1), 0), axis=-1)
    count = jnp.sum(pairs, axis=-1)
    items = jnp.where(at[:, 0] < count[:, None], items, 16 * 2048 + 32)
    return items, count


def on_device(tokens, qkv_w, out_w, gain, proj_w, up_w, conv_w, conv_b, lists, counts):
    x = lax.axis_index("x")
    z = lax.axis_index("z")
    strip = lax.axis_index("head")
    flat = tokens.reshape(-1, D)
    right = [(i, (i + 1) % 4) for i in range(4)]
    left = [(i, (i - 1) % 4) for i in range(4)]
    packed = qkv(flat, qkv_w)
    packed, lists, counts = lax.optimization_barrier((packed, lists, counts))
    items, cnt = local_items(lists, counts, x, z)
    packed = lax.all_to_all(packed, "head", split_axis=0, concat_axis=0, tiled=True)
    q = packed[:, :128]
    kv = packed[:, 128:]
    kv_far = lax.ppermute(kv, "z", [(0, 1), (1, 0)])
    q1 = lax.ppermute(q, "x", right)
    q3 = lax.ppermute(q, "x", left)
    q2a = lax.ppermute(q1[:8], "x", right)
    q2b = lax.ppermute(q3[8:], "x", left)
    info = (x - jnp.arange(4, dtype=jnp.int32)) % 4
    part = attend((0, 1, 3), items, cnt, info, kv, kv_far, [q, q1, q3])
    last = attend((2,), items, cnt, info, kv, kv_far, [q2a, q2b])
    part = lax.dynamic_update_slice_in_dim(part, last, info[2], 0)
    part = lax.all_to_all(
        part.reshape(64, 72, 128), ("x", "head"), split_axis=0, concat_axis=0, tiled=True
    )
    feat, top, bot = mix(part, flat, out_w, gain[None, :], proj_w)
    above = lax.ppermute(bot, "head", [(i, i + 1) for i in range(15)])
    below = lax.ppermute(top, "head", [(i + 1, i) for i in range(15)])
    return dense_head(
        strip[None], feat, above, below, up_w, conv_w.reshape(2, 3, 3 * CH, CH), conv_b
    )


def solution(mesh):
    grid = Mesh(mesh.devices.reshape(2, 4, 16), ("z", "x", "head"))
    rows = ("z", "x")
    in_specs = (
        P(rows, "head", None),
        P(),
        P(),
        P(),
        P(),
        P(),
        P(),
        P(),
        P(rows, None),
        P(rows),
    )
    return jax.shard_map(
        on_device,
        mesh=grid,
        in_specs=in_specs,
        out_specs=P(rows, "head", None, None),
        check_vma=False,
    )
```

```python
import functools

import jax
import jax.numpy as jnp
from jax import lax
from jax.experimental import pallas as pl
from jax.experimental.pallas import tpu as pltpu
from jax.sharding import Mesh, PartitionSpec as P

D = 1024
HEADS = 16
HD = 64
CH = 256
SLOTS = 26
STRIP = 64
NEG = -2e38
bf16 = jnp.bfloat16
f32 = jnp.float32


def split(v):
    hi = v.astype(bf16)
    return hi, (v - hi.astype(f32)).astype(bf16)


def dot(a, b):
    return jnp.dot(a, b, preferred_element_type=f32)


def dot3(ah, al, bh, bl):
    m = ah.shape[0]
    both = dot(jnp.concatenate([ah, al], axis=0), bh)
    return both[:m] + (both[m:] + dot(ah, bl))


def lanes(shape):
    return lax.broadcasted_iota(jnp.int32, shape, len(shape) - 1)


def qkv_body(x_ref, w_ref, out_ref, xh, xl):
    @pl.when(pl.program_id(0) == 0)
    def _():
        hi, lo = split(x_ref[...])
        xh[...] = hi
        xl[...] = lo

    wh, wl = split(w_ref[...])
    r = dot3(xh[...], xl[...], wh, wl)
    for u in range(4):
        q = r[:, u * 192 : u * 192 + HD] * 0.125
        k = r[:, u * 192 + HD : u * 192 + 2 * HD]
        v = r[:, u * 192 + 2 * HD : u * 192 + 3 * HD]
        for i, t in enumerate((q, k)):
            lo = t - t.astype(bf16).astype(f32)
            out_ref[u, i * 128 : i * 128 + 128, :] = jnp.concatenate([t, lo], axis=1).astype(bf16)
        out_ref[u, 256:320, :] = jnp.concatenate([v[:STRIP], v[STRIP:]], axis=1).astype(bf16)


def qkv(x, w):
    return pl.pallas_call(
        qkv_body,
        grid=(HEADS // 4,),
        in_specs=[
            pl.BlockSpec((128, D), lambda g: (0, 0)),
            pl.BlockSpec((D, 768), lambda g: (0, g)),
        ],
        out_specs=pl.BlockSpec((4, 320, 128), lambda g: (g, 0, 0)),
        out_shape=jax.ShapeDtypeStruct((HEADS, 320, 128), bf16),
        scratch_shapes=[pltpu.VMEM((128, D), bf16), pltpu.VMEM((128, D), bf16)],
        name="qkv",
    )(x, w)


UNROLL = 12
PAIRS = 16 * (SLOTS // 2)
ROOM = PAIRS + UNROLL


def attend_body(sets, fresh, items, cnt, info, in0, in1, *refs):
    if fresh:
        kv0, kv1 = in0, in1
        qrefs, (o_ref, ks, vs, qs, sc, ms, accs) = refs[:-7], refs[-7:]
    else:
        ks, vs = in0, in1
        qrefs, (o_ref, qs, sc, ms, accs) = refs[:-5], refs[-5:]
    low = lanes((128, 128)) < HD

    def strips(ref, j, rows):
        return jnp.concatenate([ref[2 * j, rows, :], ref[2 * j + 1, rows, :]], axis=0)

    def ready(j, _):
        for fr in range(2):
            rows = slice(fr * 64, fr * 64 + 64)
            for src, kv in enumerate((kv0, kv1)):
                b = src * 16 + fr * 8 + j
                a = strips(kv, j, rows).astype(f32)
                swapped = pltpu.roll(a, 64, 1)
                ks[b, :, 0:128] = jnp.where(low, a, swapped).astype(bf16)
                ks[b, :, 128:256] = swapped.astype(bf16)
                v = strips(kv, j, slice(128, 192)).astype(f32)
                if fr:
                    v = pltpu.roll(v, 64, 1)
                vs[b] = jnp.where(low, v, 1.0).astype(bf16)
        return 0

    if fresh:
        lax.fori_loop(0, 8, ready, 0)
        vs[32] = jnp.zeros((128, 128), bf16)

    for i in range(len(sets)):
        mine = (qrefs[i],) if len(sets) > 1 else qrefs
        for part, q in enumerate(mine):

            def ready_q(j, _, i=i, part=part, q=q):
                for fr in range(2):
                    rows = slice(fr * 64, fr * 64 + 64)
                    qs[17 * i + fr * 8 + 4 * part + j] = strips(q, j, rows)
                return 0

            lax.fori_loop(0, 8 // len(mine), ready_q, 0)
        qs[17 * i + 16] = jnp.zeros((128, 128), bf16)
    eye = lax.broadcasted_iota(jnp.int32, (128, 128), 0) == lanes((128, 128))

    def clear(b, _):
        ms[b] = jnp.full((128, 128), NEG, f32)
        return 0

    lax.fori_loop(0, 17, clear, 0)
    accs[16] = jnp.zeros((128, 128), f32)

    def one_set(i, _):
        s = sets[0]
        for n in range(1, len(sets)):
            s = jnp.where(i == n, sets[n], s)
        trips = (cnt[s] + UNROLL - 1) // UNROLL

        def score(t, _):
            got = []
            for u in range(UNROLL):
                item = items[s, t * UNROLL + u]
                ia = (item >> 6) & 31
                ib = item & 63
                a = qs[17 * i + (item >> 11)]
                got.append(
                    lax.dot_general(
                        jnp.concatenate([a, a[:, :HD]], axis=1),
                        jnp.concatenate(
                            [ks[ia, :, :192], ks[jnp.where(ib == 32, ia, ib), :, :192]], axis=0
                        ),
                        (((1,), (1,)), ((), ())),
                        preferred_element_type=f32,
                    )
                )
            for u in range(UNROLL):
                qi = items[s, t * UNROLL + u] >> 11
                sc[t * UNROLL + u] = got[u]
                ms[qi] = jnp.maximum(ms[qi], jnp.maximum(got[u][:, :128], got[u][:, 128:]))
            return 0

        lax.fori_loop(0, trips, score, 0)

        def peak(b, _):
            for u in range(8):
                m = jnp.max(ms[8 * b + u], axis=1, keepdims=True)
                ms[8 * b + u] = jnp.broadcast_to(m, (128, 128))
                accs[8 * b + u] = jnp.zeros((128, 128), f32)
            return 0

        lax.fori_loop(0, 2, peak, 0)

        def blend(t, _):
            got = []
            for u in range(UNROLL):
                item = items[s, t * UNROLL + u]
                m = ms[item >> 11]
                p = jnp.exp(sc[t * UNROLL + u] - jnp.concatenate([m, m], axis=1))
                v = jnp.concatenate([vs[(item >> 6) & 31], vs[item & 63]], axis=0)
                got.append(dot(p.astype(bf16), v))
            for u in range(UNROLL):
                qi = items[s, t * UNROLL + u] >> 11
                accs[qi] = accs[qi] + got[u]
            return 0

        lax.fori_loop(0, trips, blend, 0)
        to = info[s] if len(sets) > 1 else 0

        def diagonal(v):
            return jnp.sum(jnp.where(eye, v, 0.0), axis=0, keepdims=True)

        def emit(jj, _):
            emit_one(2 * jj)
            emit_one(2 * jj + 1)
            return 0

        def emit_one(j):
            a0 = accs[j]
            a1 = accs[8 + j]
            s0 = pltpu.roll(a0, 64, 1)
            s1 = pltpu.roll(a1, 64, 1)
            total = jnp.maximum(jnp.where(low, s0, a1), 0.5)
            out = (jnp.where(low, a0, s1) / total).astype(bf16)
            l0 = jnp.maximum(diagonal(jnp.where(low, s0, a0)), 0.5)
            l1 = jnp.maximum(diagonal(jnp.where(low, s1, a1)), 0.5)
            t0 = diagonal(ms[j]) + jnp.log(l0)
            t1 = diagonal(ms[8 + j]) + jnp.log(l1)
            ms[j] = jnp.full((128, 128), NEG, f32)
            ms[8 + j] = jnp.full((128, 128), NEG, f32)
            sub = lax.broadcasted_iota(jnp.int32, (8, 128), 0)
            for half in range(2):
                o_ref[to, 2 * j + half, 0:64, :] = out[half * 64 : half * 64 + 64]
                c = half * 64
                row = jnp.concatenate([t0[:, c : c + 64], t1[:, c : c + 64]], axis=1)
                hi = row.astype(bf16).astype(f32)
                mid = (row - hi).astype(bf16).astype(f32)
                last = row - hi - mid
                tile = jnp.where(
                    sub == 0, hi, jnp.where(sub == 1, mid, jnp.where(sub == 2, last, 0.0))
                )
                o_ref[to, 2 * j + half, 64:72, :] = tile.astype(bf16)

        lax.fori_loop(0, 4, emit, 0)
        return 0

    lax.fori_loop(0, len(sets), one_set, 0)


def attend(sets, fresh, items, cnt, info, in0, in1, qs):
    smem = pl.BlockSpec(memory_space=pltpu.SMEM)
    vmem = pl.BlockSpec(memory_space=pltpu.VMEM)
    out_shape = [jax.ShapeDtypeStruct((4 if len(sets) > 1 else 1, HEADS, 72, 128), bf16)]
    if fresh:
        out_shape += [
            jax.ShapeDtypeStruct((32, 128, 256), bf16),
            jax.ShapeDtypeStruct((33, 128, 128), bf16),
        ]
    return pl.pallas_call(
        functools.partial(attend_body, sets, fresh),
        in_specs=[smem, smem, smem] + [vmem] * (2 + len(qs)),
        out_specs=[vmem] * len(out_shape),
        out_shape=out_shape,
        scratch_shapes=[
            pltpu.VMEM((17 * len(sets), 128, 128), bf16),
            pltpu.VMEM((ROOM, 128, 256), f32),
            pltpu.VMEM((17, 128, 128), f32),
            pltpu.VMEM((17, 128, 128), f32),
        ],
        compiler_params=pltpu.CompilerParams(vmem_limit_bytes=38 << 20),
    )(items, cnt, info, in0, in1, *qs)


def mix_body(r_ref, x_ref, w_ref, gain_ref, proj_ref, feat_ref, top_ref, bot_ref, att):
    lse = jnp.sum(r_ref[:, 64:72, :].astype(f32), axis=1)
    parts = [lse[16 * x : 16 * x + 16] for x in range(4)]
    peak = jnp.maximum(jnp.maximum(parts[0], parts[1]), jnp.maximum(parts[2], parts[3]))
    es = [jnp.exp(p - peak) for p in parts]
    total = (es[0] + es[1]) + (es[2] + es[3])
    share = jnp.concatenate([e / total for e in es], axis=0)
    share = jnp.concatenate([share, share], axis=0).T
    both = jnp.where(lanes((STRIP, 128)) < 64, share[:STRIP], share[STRIP:])
    bh, bl = split(both)
    low = lanes((STRIP, 128)) < HD
    row = lax.broadcasted_iota(jnp.int32, (128, 2048), 0)
    col = lanes((128, 2048))
    half = (row >= 64) == (col % 128 >= 64)
    wide = []
    for x in range(4):
        spread = jnp.where(half & (row % 64 == 16 * x + col // 128), 1.0, 0.0).astype(bf16)
        wide.append(dot(bh, spread) + dot(bl, spread))
    for p in range(HEADS // 2):
        t = []
        for h in (2 * p, 2 * p + 1):
            acc = None
            for x in range(4):
                o = r_ref[16 * x + h, 0:64, :].astype(f32) * wide[x][:, 128 * h : 128 * h + 128]
                acc = o if acc is None else acc + o
            t.append(acc)
        att[0:64, 128 * p : 128 * p + 128] = jnp.where(low, t[0], pltpu.roll(t[1], 64, 1))
        att[64:128, 128 * p : 128 * p + 128] = jnp.where(low, pltpu.roll(t[0], 64, 1), t[1])
    ah, al = split(att[...])
    wh, wl = split(w_ref[...])
    stream = x_ref[...] + dot3(ah, al, wh, wl)
    centred = stream - jnp.mean(stream, axis=1, keepdims=True)
    spread = jnp.mean(centred * centred, axis=1, keepdims=True)
    normed = centred * lax.rsqrt(spread + 1e-05) * gain_ref[...]
    nh, nl = split(normed)
    ph, plo = split(proj_ref[...])
    feat = dot3(nh, nl, ph, plo).astype(bf16)
    feat_ref[...] = feat
    for f in range(2):
        top_ref[32 * f : 32 * f + 32] = feat[64 * f : 64 * f + 32]
        bot_ref[32 * f : 32 * f + 32] = feat[64 * f + 32 : 64 * f + 64]


def mix(r, x, w, gain, proj):
    return pl.pallas_call(
        mix_body,
        out_shape=(
            jax.ShapeDtypeStruct((128, CH), bf16),
            jax.ShapeDtypeStruct((64, CH), bf16),
            jax.ShapeDtypeStruct((64, CH), bf16),
        ),
        scratch_shapes=[pltpu.VMEM((128, D), f32)],
        compiler_params=pltpu.CompilerParams(vmem_limit_bytes=20 << 20),
        name="mix",
    )(r, x, w, gain, proj)


def shifted(dst, src, rows, relu):
    def one(r, _):
        for dx in range(3):
            for half in range(2):
                v = src[half * rows + r, pl.ds(7 + dx, 128), :]
                if relu:
                    v = jnp.maximum(v, 0.0)
                dst[r, :, dx * 256 + half * 128 : dx * 256 + half * 128 + 128] = v.astype(bf16)
        return 0

    lax.fori_loop(0, rows, one, 0)


def head_body(pos, feat_ref, above_ref, below_ref, up_ref, cw_ref, cb_ref, out_ref, ups, u3, hid, h3):
    at = pos[0]

    @pl.when(pl.program_id(0) == 0)
    def _():
        for ref, rows in ((ups, 24), (hid, 20)):
            ref[:, 0:8, :] = jnp.zeros((rows, 8, 128), f32)
            ref[:, 136:144, :] = jnp.zeros((rows, 8, 128), f32)

    own = feat_ref[...]
    early = jnp.concatenate([own, below_ref[...]], axis=0)
    late = jnp.concatenate([above_ref[...], own], axis=0)
    for a in range(4):
        src = early if a < 2 else late
        lifted = dot(src, up_ref[:, 1024 * a : 1024 * a + 1024]).astype(bf16).astype(f32)
        for i in range(3):
            row = 2 + 4 * i + a if a < 2 else 4 * i + a - 2
            for e in range(4):
                for half in range(2):
                    c = 256 * e + 128 * half
                    ups[12 * half + row, pl.ds(8 + e, 32, stride=4), :] = lifted[
                        32 * i : 32 * i + 32, c : c + 128
                    ]
    shifted(u3, ups, 12, True)

    def conv1(r, _):
        acc = None
        for dy in range(3):
            part = dot(u3[pl.ds(2 * r + dy, 2)].reshape(256, 768), cw_ref[0, dy])
            acc = part if acc is None else acc + part
        h = jnp.maximum(acc + cb_ref[0:1, :], 0.0).astype(bf16).astype(f32)
        for k in range(2):
            y = 2 * r + k
            keep = ((y > 0) | (at > 0)) & ((y < 9) | (at < 15))
            v = jnp.where(keep, h[128 * k : 128 * k + 128], 0.0)
            for half in range(2):
                hid[10 * half + y, 8:136, :] = v[:, 128 * half : 128 * half + 128]
        return 0

    lax.fori_loop(0, 5, conv1, 0)
    shifted(h3, hid, 10, False)

    def conv2(r, _):
        acc = None
        for dy in range(3):
            part = dot(h3[pl.ds(2 * r + dy, 2)].reshape(256, 768), cw_ref[1, dy])
            acc = part if acc is None else acc + part
        acc = acc + cb_ref[1:2, :]
        for k in range(2):
            y = 2 * r + k
            for half in range(2):
                c = 128 * half
                v = ups[12 * half + y + 2, 8:136, :] + acc[128 * k : 128 * k + 128, c : c + 128]
                out_ref[0, y, :, c : c + 128] = v.astype(bf16)
        return 0

    lax.fori_loop(0, 4, conv2, 0)


def dense_head(pos, feat, above, below, up, cw, cb):
    whole = lambda shape: pl.BlockSpec(shape, lambda f: (0,) * len(shape))
    return pl.pallas_call(
        head_body,
        grid=(2,),
        in_specs=[
            pl.BlockSpec(memory_space=pltpu.SMEM),
            pl.BlockSpec((64, CH), lambda f: (f, 0)),
            pl.BlockSpec((32, CH), lambda f: (f, 0)),
            pl.BlockSpec((32, CH), lambda f: (f, 0)),
            whole((CH, 16 * CH)),
            whole((2, 3, 3 * CH, CH)),
            whole((2, CH)),
        ],
        out_specs=pl.BlockSpec((1, 8, 128, CH), lambda f: (f, 0, 0, 0)),
        out_shape=jax.ShapeDtypeStruct((2, 8, 128, CH), bf16),
        scratch_shapes=[
            pltpu.VMEM((24, 144, 128), f32),
            pltpu.VMEM((12, 128, 768), bf16),
            pltpu.VMEM((20, 144, 128), f32),
            pltpu.VMEM((10, 128, 768), bf16),
        ],
        compiler_params=pltpu.CompilerParams(vmem_limit_bytes=24 << 20),
        name="dense_head",
    )(pos, feat, above, below, up, cw, cb)


def local_items(lists, counts, x, z):
    packed = jnp.concatenate([lists, counts[:, None]], axis=1)
    sets = [packed] + [
        lax.ppermute(packed, "x", [(i, (i + k) % 4) for i in range(4)]) for k in (1, 2, 3)
    ]
    packed = jnp.stack(sets, axis=0)
    ids = packed[:, :, :SLOTS]
    slot = jnp.arange(SLOTS, dtype=jnp.int32)
    block = jnp.arange(16, dtype=jnp.int32)
    mine = (slot < packed[:, :, SLOTS:]) & ((ids // 16) % 4 == x)
    local = jnp.where(ids // 64 == z, 0, 16) + ids % 16
    ones = mine.astype(jnp.int32)
    inside = jnp.sum(jnp.where(slot[None, :] < slot[:, None], ones[:, :, None, :], 0), axis=-1)
    total = jnp.sum(ones, axis=-1)
    pairs = (total + 1) // 2
    ahead = jnp.sum(jnp.where(block[None, :] < block[:, None], pairs[:, None, :], 0), axis=-1)
    place = jnp.where(mine, ahead[:, :, None] + inside // 2, -1).reshape(4, 1, -1)
    alone = jnp.where(inside + 1 == total[:, :, None], 32, 0)
    value = jnp.where(inside % 2 == 0, block[:, None] * 2048 + local * 64 + alone, local)
    at = jnp.arange(ROOM, dtype=jnp.int32)[:, None]
    items = jnp.sum(jnp.where(place == at, value.reshape(4, 1, -1), 0), axis=-1)
    count = jnp.sum(pairs, axis=-1)
    items = jnp.where(at[:, 0] < count[:, None], items, 16 * 2048 + 32)
    return items, count


def on_device(tokens, qkv_w, out_w, gain, proj_w, up_w, conv_w, conv_b, lists, counts):
    x = lax.axis_index("x")
    z = lax.axis_index("z")
    strip = lax.axis_index("head")
    flat = tokens.reshape(-1, D)
    right = [(i, (i + 1) % 4) for i in range(4)]
    left = [(i, (i - 1) % 4) for i in range(4)]
    packed = qkv(flat, qkv_w)
    packed, lists, counts = lax.optimization_barrier((packed, lists, counts))
    items, cnt = local_items(lists, counts, x, z)
    packed = lax.all_to_all(packed, "head", split_axis=0, concat_axis=0, tiled=True)
    q = packed[:, :128]
    kv = packed[:, 128:]
    kv_far = lax.ppermute(kv, "z", [(0, 1), (1, 0)])
    q1 = lax.ppermute(q, "x", right)
    q3 = lax.ppermute(q, "x", left)
    q2a = lax.ppermute(q1[:8], "x", right)
    q2b = lax.ppermute(q3[8:], "x", left)
    info = (x - jnp.arange(4, dtype=jnp.int32)) % 4
    part, ks, vs = attend((0, 1, 3), True, items, cnt, info, kv, kv_far, [q, q1, q3])
    (last,) = attend((2,), False, items, cnt, info, ks, vs, [q2a, q2b])
    part = lax.dynamic_update_slice_in_dim(part, last, info[2], 0)
    part = lax.all_to_all(
        part.reshape(64, 72, 128), ("x", "head"), split_axis=0, concat_axis=0, tiled=True
    )
    feat, top, bot = mix(part, flat, out_w, gain[None, :], proj_w)
    above = lax.ppermute(bot, "head", [(i, i + 1) for i in range(15)])
    below = lax.ppermute(top, "head", [(i + 1, i) for i in range(15)])
    return dense_head(
        strip[None], feat, above, below, up_w, conv_w.reshape(2, 3, 3 * CH, CH), conv_b
    )


def solution(mesh):
    grid = Mesh(mesh.devices.reshape(2, 4, 16), ("z", "x", "head"))
    rows = ("z", "x")
    in_specs = (
        P(rows, "head", None),
        P(),
        P(),
        P(),
        P(),
        P(),
        P(),
        P(),
        P(rows, None),
        P(rows),
    )
    return jax.shard_map(
        on_device,
        mesh=grid,
        in_specs=in_specs,
        out_specs=P(rows, "head", None, None),
        check_vma=False,
    )
```
